32 devices in a mesh: row: 4 (over z), col: 8 (over y, x, core).
Axes of the slice: x: 2, y: 2, z: 4, core: 2. Of those that a mesh axis runs over, the one named last changes fastest.
Arguments:
- hamiltonian: bfloat16 [2048, 2048], P('row', 'col'), may hold values from -0.3 to 0.3
- pattern: int32 [16, 16], replicated, may hold values from 0 to 1, as said below
- tile_lists: int32 [32, 8], replicated, may hold values from 0 to 15, as said below
- orders: int32 [32], replicated, may hold values from 6 to 8
- shift: float32 [1], replicated, may hold values from -0.5 to 0.5
Outputs:
- density: bfloat16 [2048, 2048], P('row', 'col')
- php: float32 [2048, 2048], P('row', 'col')
The draws below stay inside these ranges and needn't reach their ends.
Inputs may be any that keep to these rules, and one draw needn't show every extreme that they name: `pattern`: Symmetric, with zeros on the diagonal. `tile_lists`: row s begins with tile s * 64 // 128; its entries lie in distinct groups of 2 consecutive tiles, and the second lies in the group that shares a group of 4 consecutive tiles with the first. Entries from position orders[s] on are not used.
All inputs are finite; a program needn't handle non-finite values.
Results may differ from the reference program's by a relative error of at most 0.0073.
Values may be sent and summed in bfloat16 or wider, within the bound.
A program may use at most 64 MiB of HBM per device.

```python
import jax
import jax.numpy as jnp
from jax import lax

TILE = 128
TPC = 2
MAXT = 8
MINT = 6
ITERS = 3
NB = 16
NH = 2048
SUBS = 32
CW = 64


def draw_hamiltonian(key, part):
    raw = jax.random.truncated_normal(key, -4.0, 4.0, (NH, NH), jnp.float32) * 0.05
    mirrored = (raw + raw.T) * 0.5 ** 0.5
    return mirrored.astype(jnp.bfloat16)


def draw_pattern(key, part):
    picks = jax.random.randint(jax.random.fold_in(key, 5), (NB, NB), 0, 4, dtype=jnp.int32)
    upper = jnp.triu((picks == 0).astype(jnp.int32), 1)
    return (upper + upper.T).astype(jnp.int32)


def one_list(key, index):
    groups = NB // TPC
    center = index * CW // TILE
    home = center // TPC
    partner = jnp.bitwise_xor(home, 1)
    scores = jax.random.permutation(jax.random.fold_in(key, 7), groups).astype(jnp.int32)
    positions = jnp.arange(groups, dtype=jnp.int32)
    scores = jnp.where(positions == home, -2, scores)
    scores = jnp.where(positions == partner, -1, scores)
    chosen = jnp.argsort(scores, stable=True)[:MAXT].astype(jnp.int32)
    offsets = jax.random.randint(jax.random.fold_in(key, 11), (MAXT,), 0, TPC, dtype=jnp.int32)
    tiles = chosen * TPC + offsets
    return tiles.at[0].set(center.astype(jnp.int32))


def draw_tile_lists(key, part):
    keys = jax.random.split(jax.random.fold_in(key, 3), SUBS)
    return jax.vmap(one_list)(keys, jnp.arange(SUBS, dtype=jnp.int32)).astype(jnp.int32)


def with_ends(values, rng, smallest, top_value):
    longest = values.shape.index(max(values.shape))
    spots = []
    for shift in (0, 1):
        where = [jax.random.randint(jax.random.fold_in(rng, axis), (), 0, length) for axis, length in enumerate(values.shape)]
        where[longest] = (where[longest] + shift) % values.shape[longest]
        spots.append(tuple(where))
    return values.at[spots[0]].set(smallest).at[spots[1]].set(top_value)


def setup_inputs(seed: int = 0) -> dict:
    key_of = jax.random.split(jax.random.key(seed), 6)
    hamiltonian = draw_hamiltonian(jax.random.fold_in(key_of[5], 71), 0)
    pattern = draw_pattern(jax.random.fold_in(key_of[5], 71), 0)
    tile_lists = draw_tile_lists(jax.random.fold_in(key_of[5], 71), 0)
    orders = with_ends(jax.random.randint(key_of[3], (SUBS,), MINT, MAXT + 1), jax.random.fold_in(key_of[3], 1), MINT, MAXT).astype(jnp.int32)
    shift = jnp.clip(jax.random.uniform(key_of[4], (1,), jnp.float32, -0.5, 0.5), -0.5, 0.5)
    return {"hamiltonian": hamiltonian, "pattern": pattern, "tile_lists": tile_lists, "orders": orders, "shift": shift}


def masked_blocks(hamiltonian, pattern):
    count = pattern.shape[0]
    keep = jnp.maximum(pattern, jnp.eye(count, dtype=jnp.int32))
    blocks = hamiltonian.reshape(count, TILE, count, TILE).transpose(0, 2, 1, 3)
    return jnp.where(keep[:, :, None, None] > 0, blocks, jnp.zeros_like(blocks))

def newton_density(sub, live_rows, potential):
    eye = jnp.eye(sub.shape[0], dtype=jnp.float32)
    shifted = sub.astype(jnp.float32) - potential * eye * live_rows[None, :]
    row_squares = lax.optimization_barrier(jnp.sum(shifted * shifted, axis=1))
    scale = jnp.abs(potential) + 2.0 * jnp.sqrt(jnp.max(row_squares) + 1e-06)
    iterate = (shifted / scale).astype(jnp.bfloat16)
    product = shifted
    for step in range(ITERS):
        square = jnp.dot(iterate, iterate, preferred_element_type=jnp.float32)
        factor = (1.5 * eye - 0.5 * square).astype(jnp.bfloat16)
        product = jnp.dot(iterate, factor, preferred_element_type=jnp.float32)
        if step + 1 < ITERS:
            iterate = product.astype(jnp.bfloat16)
    return 0.5 * (eye - product)

def reference(hamiltonian, pattern, tile_lists, orders, shift):
    count = pattern.shape[0]
    blocks = masked_blocks(hamiltonian, pattern)
    potential = shift[0]
    total = tile_lists.shape[0]
    width = count * TILE // total

    def solve(index):
        tiles = tile_lists[index]
        live = jnp.arange(MAXT, dtype=jnp.int32) < orders[index]
        sub = jnp.take(jnp.take(blocks, tiles, axis=0), tiles, axis=1)
        both = live[:, None] & live[None, :]
        sub = jnp.where(both[:, :, None, None], sub, jnp.zeros_like(sub))
        sub = sub.transpose(0, 2, 1, 3).reshape(MAXT * TILE, MAXT * TILE)
        live_rows = jnp.repeat(live.astype(jnp.float32), TILE)
        dens = newton_density(sub, live_rows, potential)
        offset = (index * width % TILE).astype(jnp.int32)
        central = lax.dynamic_slice_in_dim(dens, offset, width, 1).astype(jnp.bfloat16)
        central = central.astype(jnp.float32).reshape(MAXT, TILE, width)
        chooser = ((tiles[:, None] == jnp.arange(count, dtype=jnp.int32)[None, :]) & live[:, None]).astype(jnp.float32)
        placed = jnp.einsum('ia,itw->atw', chooser, central)
        return placed.astype(jnp.bfloat16)
    pieces = lax.map(solve, jnp.arange(total, dtype=jnp.int32))
    density = pieces.transpose(1, 2, 0, 3).reshape(count * TILE, total * width)
    ham = blocks.transpose(0, 2, 1, 3).reshape(count * TILE, count * TILE)
    hp = jnp.dot(ham, density, preferred_element_type=jnp.float32).astype(jnp.bfloat16)
    php = jnp.dot(density, hp, preferred_element_type=jnp.float32)
    return (density, php)
```

```python
import functools

import jax
import jax.numpy as jnp
from jax import lax
from jax.experimental import pallas as pl
from jax.experimental.pallas import tpu as pltpu
from jax.sharding import PartitionSpec as P

TILE = 128
TPC = 2
MAXT = 8
BF = jnp.bfloat16
F32 = jnp.float32
MESH = pl.DeviceIdType.MESH
SPAN = MAXT * TILE
HALF = TPC * TILE


def eye_block(rows, cols, shift):
    r = lax.broadcasted_iota(jnp.int32, (rows, cols), 0)
    c = lax.broadcasted_iota(jnp.int32, (rows, cols), 1)
    return r == c + shift


def symmetric(left, right, out, finish):
    for n in range(SPAN // HALF):
        cols = slice(n * HALF, (n + 1) * HALF)
        prod = jnp.dot(left[0:(n + 1) * HALF, :], right[:, cols], preferred_element_type=F32)
        done = finish(prod, n)
        out[0:(n + 1) * HALF, cols] = done
        if n:
            out[cols, 0:n * HALF] = done[0:n * HALF, :].T


def kernel(
    rows_n, cols_n, code, lists, orders, pattern, shift, ham,
    dens_out, php_out,
    hful, xa, xb, fb, cent, call, pall, ptc, ptr, hpt,
    z_s, z_r, ze_s, ze_r, an_s, an_r, ap_s, ap_r, cz_s, cz_r, pn_s, pn_r, pp_s, pp_r,
):
    me_row = lax.axis_index("row")
    me_col = lax.axis_index("col")
    high, wide = ham.shape
    gpr = high // HALF
    groups = rows_n * gpr
    width = wide // rows_n
    pairs_n = cols_n // 2
    bits = pairs_n.bit_length() - 1
    my_pair = me_col // 2
    parity = lax.rem(me_col, 2)
    partner = my_pair * 2 + 1 - parity
    solver = me_col * rows_n + me_row

    def send(src, dst, ss, rs, row, col):
        return pltpu.make_async_remote_copy(
            src_ref=src, dst_ref=dst, send_sem=ss, recv_sem=rs,
            device_id=(row, col), device_id_type=MESH,
        )

    barrier = pltpu.get_barrier_semaphore()
    for d in range(1, rows_n):
        pl.semaphore_signal(
            barrier, inc=1, device_id=(lax.rem(me_row + d, rows_n), me_col), device_id_type=MESH)
    for d in range(1, cols_n):
        pl.semaphore_signal(
            barrier, inc=1, device_id=(me_row, lax.rem(me_col + d, cols_n)), device_id_type=MESH)
    pl.semaphore_wait(barrier, rows_n - 1 + cols_n - 1)

    def first(q, c):
        p = c // 2
        par = lax.rem(c, 2)
        return jnp.where(q == p, 0, jnp.where(q < p, par, 1 - par))

    def flip(e, par):
        out = 0
        for j in range(bits):
            b = lax.rem(my_pair // (1 << j), 2)
            c0, c1 = (e >> j) & 1, (e >> (bits - 1 - j)) & 1
            if c0 == c1:
                b = 1 - b if c0 else b
            else:
                t = 1 - par if c0 else par
                b = b + t - 2 * b * t
            out = out + (1 << j) * b
        return out

    def column(e, par):
        return flip(e, par) * 2 + par

    def later(e):
        return [i for i in range(bits) if (1 << i) > e]

    def strip_rows(g):
        return pl.ds(g * TPC, TPC)

    steps = [0, 1, rows_n - 1] + list(range(2, rows_n - 1))

    def group_of(t, c):
        if t == rows_n:
            return c
        q = lax.rem(me_row + rows_n - steps[t], rows_n)
        return q * gpr + first(q, c)

    def block(t, c):
        return hful.at[c, strip_rows(group_of(t, c))]

    def turn(t, c):
        g = group_of(t, c)

        @pl.when(g != c)
        def _():
            hful[g, strip_rows(c)] = hful[c, strip_rows(g)].reshape(HALF, HALF).T.reshape(TPC, TILE, HALF)

    def net(src, dst, ss, rs, e, t, i):
        f = e | (1 << i)
        return send(src, dst, ss.at[f, t], rs.at[f, t], me_row, column(1 << i, parity))

    def pass_on(src, dst, ss, rs, e, t):
        return send(src, dst, ss.at[e, t], rs.at[e, t], me_row, partner)

    def forward(src, dst, sems, e, t):
        ns, nr, ps, pr = sems
        for i in later(e):
            net(src, dst, ns, nr, e, t, i).start()
        pass_on(src, dst, ps, pr, e, t).start()

    def from_net(where, sems, e, t):
        ns, nr, ps, pr = sems
        c = column(e, parity)
        ref = where(t, c)
        top = e.bit_length() - 1
        net(ref, ref, ns, nr, e ^ (1 << top), t, top).wait_recv()
        forward(ref, ref, sems, e, t)
        return c

    def from_partner(where, sems, e, t):
        ns, nr, ps, pr = sems
        c = column(e, 1 - parity)
        ref = where(t, c)
        pass_on(ref, ref, ps, pr, e, t).wait_recv()
        return c

    def drain(ref, sems, t):
        ns, nr, ps, pr = sems
        for e in range(pairs_n):
            for i in later(e):
                net(ref, ref, ns, nr, e, t, i).wait_send()
            pass_on(ref, ref, ps, pr, e, t).wait_send()

    a_sems = (an_s, an_r, ap_s, ap_r)

    def keep_own(half, g):
        for a in range(TPC):
            for b in range(TPC):
                ga = g * TPC + a
                gb = me_col * TPC + b
                keep = (pattern[ga, gb] == 1) | (ga == gb)
                t = ham[pl.ds(pl.multiple_of(half * HALF + a * TILE, TILE), TILE),
                        b * TILE:(b + 1) * TILE]
                hful[me_col, g * TPC + a, :, b * TILE:(b + 1) * TILE] = jnp.where(
                    keep, t, jnp.zeros_like(t))

    my_half = first(me_row, me_col)
    keep_own(my_half, me_row * gpr + my_half)
    own = block(0, me_col)

    def z_copy(d):
        return send(own, own, z_s.at[d], z_r.at[d], lax.rem(me_row + d, rows_n), me_col)

    def z_in(t):
        d = steps[t]
        ref = block(t, me_col)
        return send(ref, ref, z_s.at[d], z_r.at[d], lax.rem(me_row + d, rows_n), me_col)

    forward(own, own, a_sems, 0, 0)
    for d in steps[1:]:
        z_copy(d).start()
    away = lax.rem(me_row - my_pair + rows_n, rows_n)
    extra = block(rows_n, me_col)

    def ze_copy(d):
        return send(extra, extra, ze_s.at[d], ze_r.at[d], lax.rem(me_row + d, rows_n), me_col)

    @pl.when((parity == 1) & (away == 0))
    def _():
        keep_own(1, me_col)
        for d in steps[1:]:
            ze_copy(d).start()
    turn(0, me_col)

    def arrivals(t):
        for e in range(1, pairs_n):
            turn(t, from_net(block, a_sems, e, t))

    def handed(t):
        for e in range(pairs_n):
            turn(t, from_partner(block, a_sems, e, t))

    for t in range(1, rows_n):
        z_in(t).wait_recv()
        ref = block(t, me_col)
        forward(ref, ref, a_sems, 0, t)
        turn(t, me_col)
        arrivals(t - 1)
        if t > 1:
            handed(t - 2)

    @pl.when(parity == 1)
    def _():
        @pl.when(away > 0)
        def _():
            send(extra, extra, ze_s.at[away], ze_r.at[away], me_row, partner).wait_recv()
        forward(extra, extra, a_sems, 0, rows_n)
    arrivals(rows_n - 1)
    if rows_n > 1:
        handed(rows_n - 2)

    @pl.when(parity == 1)
    def _():
        for e in range(1, pairs_n):
            from_net(block, a_sems, e, rows_n)
    handed(rows_n - 1)

    @pl.when(parity == 0)
    def _():
        for e in range(pairs_n):
            from_partner(block, a_sems, e, rows_n)

    potential = shift[0]
    order = orders[solver]
    biggest = jnp.zeros((TILE, 1), F32)
    on_diag = eye_block(TILE, TILE, 0)
    for i in range(MAXT):
        ti = lists[solver, i]
        total = jnp.zeros((TILE, TILE), F32)
        for j in range(MAXT):
            tj = lists[solver, j]
            both = hful[tj // TPC, ti]
            w = jnp.where(lax.rem(tj, TPC) == 1, both[:, TILE:], both[:, :TILE])
            w = jnp.where((i < order) & (j < order), w, jnp.zeros_like(w))
            v = w.astype(F32)
            if i == j:
                move = jnp.where(i < order, potential, 0.0)
                v = v - jnp.where(on_diag, move, 0.0)
                w = v.astype(BF)
            xa[i * TILE:(i + 1) * TILE, j * TILE:(j + 1) * TILE] = w
            total = total + v * v
        biggest = jnp.maximum(biggest, jnp.sum(total, axis=1, keepdims=True))
    top = jnp.max(biggest, axis=0, keepdims=True)
    scale = jnp.abs(potential) + 2.0 * jnp.sqrt(top + 1e-06)
    inverse = 1.0 / scale
    lead = 1.5 * inverse
    tail = 0.5 * inverse * inverse * inverse

    def plain(prod, n):
        return prod.astype(BF)

    def upper(ref, n):
        return ref[0:(n + 1) * HALF, n * HALF:(n + 1) * HALF].astype(F32)

    symmetric(xa, xa, fb, plain)
    symmetric(xa, fb, xb, lambda prod, n: (lead * upper(xa, n) - tail * prod).astype(BF))
    symmetric(xb, xb, fb, plain)
    symmetric(xb, fb, xa, lambda prod, n: (1.5 * upper(xb, n) - 0.5 * prod).astype(BF))

    offset = pl.multiple_of(lax.rem(solver * width, TILE), width)
    hit = lax.broadcasted_iota(jnp.int32, (width, SPAN), 0) + offset == lax.broadcasted_iota(
        jnp.int32, (width, SPAN), 1)
    part = xa[pl.ds(offset, width), :]
    q = jnp.dot(part, xa[...], preferred_element_type=F32)
    f = (jnp.where(hit, 1.5, 0.0) - 0.5 * q).astype(BF)
    y = jnp.dot(f, xa[...], preferred_element_type=F32)
    dens = (0.5 * (jnp.where(hit, 1.0, 0.0) - y)).astype(BF)
    for i in range(MAXT):
        cent[i] = dens[:, i * TILE:(i + 1) * TILE]

    my_rows = pl.ds(pl.multiple_of(me_row * width, width), width)

    def place(g, carry):
        where = code[solver, g]
        t = cent[jnp.maximum(where, 0) // 2]
        call[g, my_rows, :] = jnp.where(where >= 0, t, jnp.zeros_like(t))
        return carry
    lax.fori_loop(0, groups, place, 0)

    def cz_copy(e, d):
        to = lax.rem(me_row + d, rows_n)
        part = lax.rem(me_row + d + e, rows_n)
        ref = call.at[pl.ds(part * gpr, gpr), my_rows, :]
        return send(ref, ref, cz_s.at[e, d], cz_r.at[e, d], to, me_col)

    for e in range(rows_n):
        for d in steps[1:]:
            cz_copy(e, d).start()

    p_sems = (pn_s, pn_r, pp_s, pp_r)

    def strip_of(t, c):
        return pall.at[c, t]

    for d in range(1, rows_n):
        cz_copy(0, d).wait_recv()
    for u in range(gpr):
        forward(call.at[me_row * gpr + u], strip_of(u, me_col), p_sems, 0, u)

    def halves(v, s, g, rows, store):
        cd = code[s, g]
        for h in range(TPC):
            ok = (cd >= 0) & (lax.rem(jnp.maximum(cd, 0), 2) == h)
            store(rows, h, jnp.where(ok, v, jnp.zeros_like(v)))

    def spread(src, c, u):
        for q in range(rows_n):
            def store(rows, h, v):
                ptr[pl.ds(pl.multiple_of(c * wide + q * width, width), width),
                    u * HALF + h * TILE:u * HALF + (h + 1) * TILE] = v
            halves(src[q * width:(q + 1) * width, :], c * rows_n + q, me_row * gpr + u, None, store)

    def own_strip(e):
        for u in range(gpr):
            g = lax.rem(me_row + e, rows_n) * gpr + u
            for q in range(rows_n):
                def store(rows, h, v):
                    ptc[g, q * width:(q + 1) * width, h * TILE:(h + 1) * TILE] = v
                halves(call[g, q * width:(q + 1) * width, :], me_col * rows_n + q, g, None, store)

    own_strip(0)
    for u in range(gpr):
        spread(call.at[me_row * gpr + u], me_col, u)
        dens_out[u * HALF:(u + 1) * HALF, :] = ptc[me_row * gpr + u].T
    near = []
    for e in range(1, pairs_n):
        for u in range(gpr):
            near.append((from_net(strip_of, p_sems, e, u), u))
    for c, u in near:
        spread(pall.at[c, u], c, u)
    for e in range(pairs_n):
        for u in range(gpr):
            c = from_partner(strip_of, p_sems, e, u)
            spread(pall.at[c, u], c, u)
    for e in range(1, rows_n):
        for d in range(1, rows_n):
            cz_copy(e, d).wait_recv()
        own_strip(e)

    def strip_product(h, carry):
        total = jnp.zeros((wide, HALF), F32)
        for g in range(groups):
            total = total + jnp.dot(
                ptc[g], hful[h, g * TPC:(g + 1) * TPC].reshape(HALF, HALF), preferred_element_type=F32)
        hpt[:, pl.ds(pl.multiple_of(h * HALF, HALF), HALF)] = total.astype(BF)
        return carry
    lax.fori_loop(0, groups, strip_product, 0)
    for u in range(gpr):
        php_out[u * HALF:(u + 1) * HALF, :] = jnp.dot(
            hpt[...], ptr[:, u * HALF:(u + 1) * HALF], preferred_element_type=F32).T

    for t in range(rows_n):
        drain(own, a_sems, t)

    @pl.when(parity == 1)
    def _():
        drain(own, a_sems, rows_n)
        @pl.when(away == 0)
        def _():
            for d in steps[1:]:
                ze_copy(d).wait_send()
    for d in steps[1:]:
        z_copy(d).wait_send()
    for u in range(gpr):
        drain(strip_of(u, me_col), p_sems, u)
    for e in range(rows_n):
        for d in range(1, rows_n):
            cz_copy(e, d).wait_send()


def per_device(hamiltonian, pattern, tile_lists, orders, shift):
    rows_n = lax.axis_size("row")
    cols_n = lax.axis_size("col")
    high, wide = hamiltonian.shape
    gpr = high // HALF
    groups = rows_n * gpr
    width = wide // rows_n
    pairs_n = cols_n // 2
    steps = jnp.arange(MAXT, dtype=jnp.int32)
    g = jnp.arange(groups, dtype=jnp.int32)
    hit = (tile_lists[:, None, :] // TPC == g[None, :, None]) & (
        steps[None, None, :] < orders[:, None, None])
    code = jnp.max(
        jnp.where(hit, steps[None, None, :] * TPC + tile_lists[:, None, :] % TPC, -1), axis=2)
    dma = pltpu.SemaphoreType.DMA
    smem = pl.BlockSpec(memory_space=pltpu.SMEM)
    vmem = pl.BlockSpec(memory_space=pltpu.VMEM)
    order = rows_n * high
    return pl.pallas_call(
        functools.partial(kernel, rows_n, cols_n),
        out_shape=(
            jax.ShapeDtypeStruct((high, wide), BF),
            jax.ShapeDtypeStruct((high, wide), F32),
        ),
        in_specs=[smem] * 5 + [vmem],
        out_specs=(vmem, vmem),
        scratch_shapes=[
            pltpu.VMEM((cols_n, order // TILE, TILE, wide), BF),
            pltpu.VMEM((SPAN, SPAN), BF),
            pltpu.VMEM((SPAN, SPAN), BF),
            pltpu.VMEM((SPAN, SPAN), BF),
            pltpu.VMEM((MAXT, width, TILE), BF),
            pltpu.VMEM((groups, wide, TILE), BF),
            pltpu.VMEM((cols_n, gpr, wide, TILE), BF),
            pltpu.VMEM((groups, wide, HALF), BF),
            pltpu.VMEM((order, high), BF),
            pltpu.VMEM((wide, order), BF),
            *[dma((rows_n,))] * 4,
            *[dma((pairs_n, rows_n + 1))] * 4,
            *[dma((rows_n, rows_n))] * 2,
            *[dma((pairs_n, gpr))] * 4,
        ],
        compiler_params=pltpu.CompilerParams(
            collective_id=0, has_side_effects=True, vmem_limit_bytes=60000000),
    )(code, tile_lists, orders, pattern, shift, hamiltonian)


def solution(mesh):
    in_specs = (P("row", "col"), P(), P(), P(), P())
    out_specs = (P("row", "col"), P("row", "col"))
    return jax.shard_map(
        per_device, mesh=mesh, in_specs=in_specs, out_specs=out_specs, check_vma=False
    )
```

```python
import functools

import jax
import jax.numpy as jnp
from jax import lax
from jax.experimental import pallas as pl
from jax.experimental.pallas import tpu as pltpu
from jax.sharding import PartitionSpec as P

TILE = 128
TPC = 2
MAXT = 8
BF = jnp.bfloat16
F32 = jnp.float32
MESH = pl.DeviceIdType.MESH
SPAN = MAXT * TILE
HALF = TPC * TILE


def eye_block(rows, cols, shift):
    r = lax.broadcasted_iota(jnp.int32, (rows, cols), 0)
    c = lax.broadcasted_iota(jnp.int32, (rows, cols), 1)
    return r == c + shift


def symmetric(left, right, out, finish):
    for n in range(SPAN // HALF):
        cols = slice(n * HALF, (n + 1) * HALF)
        prod = jnp.dot(left[0:(n + 1) * HALF, :], right[:, cols], preferred_element_type=F32)
        done = finish(prod, n)
        out[0:(n + 1) * HALF, cols] = done
        if n:
            out[cols, 0:n * HALF] = done[0:n * HALF, :].T


def kernel(
    rows_n, cols_n, code, lists, orders, pattern, shift, ham,
    dens_out, php_out,
    hful, xa, xb, fb, cent, call, pall, ptc, ptr, acc, hpt,
    zu_s, zd_s, z_r, ze_s, ze_r, an_s, an_r, ap_s, ap_r, cd_s, cu_s, cl_s, c_r,
    pn_s, pn_r, pp_s, pp_r,
):
    me_row = lax.axis_index("row")
    me_col = lax.axis_index("col")
    high, wide = ham.shape
    gpr = high // HALF
    groups = rows_n * gpr
    width = wide // rows_n
    pairs_n = cols_n // 2
    bits = pairs_n.bit_length() - 1
    my_pair = me_col // 2
    parity = lax.rem(me_col, 2)
    partner = my_pair * 2 + 1 - parity
    solver = me_col * rows_n + me_row

    def send(src, dst, ss, rs, row, col):
        return pltpu.make_async_remote_copy(
            src_ref=src, dst_ref=dst, send_sem=ss, recv_sem=rs,
            device_id=(row, col), device_id_type=MESH,
        )

    barrier = pltpu.get_barrier_semaphore()
    for d in range(1, rows_n):
        pl.semaphore_signal(
            barrier, inc=1, device_id=(lax.rem(me_row + d, rows_n), me_col), device_id_type=MESH)
    for d in range(1, cols_n):
        pl.semaphore_signal(
            barrier, inc=1, device_id=(me_row, lax.rem(me_col + d, cols_n)), device_id_type=MESH)
    pl.semaphore_wait(barrier, rows_n - 1 + cols_n - 1)

    def first(q, c):
        p = c // 2
        par = lax.rem(c, 2)
        return jnp.where(q == p, 0, jnp.where(q < p, par, 1 - par))

    def flip(e, par):
        out = 0
        for j in range(bits):
            b = lax.rem(my_pair // (1 << j), 2)
            c0, c1 = (e >> j) & 1, (e >> (bits - 1 - j)) & 1
            if c0 == c1:
                b = 1 - b if c0 else b
            else:
                t = 1 - par if c0 else par
                b = b + t - 2 * b * t
            out = out + (1 << j) * b
        return out

    def column(e, par):
        return flip(e, par) * 2 + par

    def later(e):
        return [i for i in range(bits) if (1 << i) > e]

    def strip_rows(g):
        return pl.ds(g * TPC, TPC)

    below = jnp.where(me_row < rows_n - 1 - me_row, me_row, rows_n - 1 - me_row)
    rest = jnp.where(me_row < rows_n - 1 - me_row, 1, -1)

    def row_at(t):
        near = me_row + (t + 1) // 2 if t % 2 else me_row - t // 2
        return jnp.where(t <= 2 * below, near, me_row + rest * (t - below))

    def group_of(q, c):
        if q is rows_n:
            return c
        return q * gpr + first(q, c)

    def block(q, c):
        return hful.at[c, strip_rows(group_of(q, c))]

    def turn(q, c):
        g = group_of(q, c)

        @pl.when(g != c)
        def _():
            hful[g, strip_rows(c)] = hful[c, strip_rows(g)].reshape(HALF, HALF).T.reshape(
                TPC, TILE, HALF)

    def net(src, dst, ss, rs, e, t, i):
        f = e | (1 << i)
        return send(src, dst, ss.at[f, t], rs.at[f, t], me_row, column(1 << i, parity))

    def pass_on(src, dst, ss, rs, e, t):
        return send(src, dst, ss.at[e, t], rs.at[e, t], me_row, partner)

    def forward(src, dst, sems, e, t):
        ns, nr, ps, pr = sems
        for i in later(e):
            net(src, dst, ns, nr, e, t, i).start()
        pass_on(src, dst, ps, pr, e, t).start()

    def from_net(where, sems, e, t):
        ns, nr, ps, pr = sems
        c = column(e, parity)
        ref = where(t, c)
        top = e.bit_length() - 1
        net(ref, ref, ns, nr, e ^ (1 << top), t, top).wait_recv()
        forward(ref, ref, sems, e, t)
        return c

    def from_partner(where, sems, e, t):
        ns, nr, ps, pr = sems
        c = column(e, 1 - parity)
        ref = where(t, c)
        pass_on(ref, ref, ps, pr, e, t).wait_recv()
        return c

    def drain(ref, sems, t):
        ns, nr, ps, pr = sems
        for e in range(pairs_n):
            for i in later(e):
                net(ref, ref, ns, nr, e, t, i).wait_send()
            pass_on(ref, ref, ps, pr, e, t).wait_send()

    a_sems = (an_s, an_r, ap_s, ap_r)

    def keep_own(half, g):
        for a in range(TPC):
            for b in range(TPC):
                ga = g * TPC + a
                gb = me_col * TPC + b
                keep = (pattern[ga, gb] == 1) | (ga == gb)
                t = ham[pl.ds(pl.multiple_of(half * HALF + a * TILE, TILE), TILE),
                        b * TILE:(b + 1) * TILE]
                hful[me_col, g * TPC + a, :, b * TILE:(b + 1) * TILE] = jnp.where(
                    keep, t, jnp.zeros_like(t))

    my_half = first(me_row, me_col)
    keep_own(my_half, me_row * gpr + my_half)

    def along(ref, ss, rs, sign):
        return send(ref, ref, ss, rs, me_row + sign, me_col)

    def relay(q, make):
        @pl.when((q <= me_row) & (me_row < rows_n - 1))
        def _():
            make(1)

        @pl.when((q >= me_row) & (me_row > 0))
        def _():
            make(-1)

    def z_copy(q, sign):
        return along(block(q, me_col), (zu_s if sign > 0 else zd_s).at[q], z_r.at[q], sign)

    def z_send(q):
        relay(q, lambda sign: z_copy(q, sign).start())

    extra = block(rows_n, me_col)

    def ze_copy(sign):
        return along(extra, ze_s.at[(sign + 1) // 2], ze_r, sign)

    own = block(me_row, me_col)
    z_send(me_row)
    forward(own, own, a_sems, 0, me_row)

    @pl.when((parity == 1) & (me_row == my_pair))
    def _():
        keep_own(1, me_col)
        relay(my_pair, lambda sign: ze_copy(sign).start())
    turn(me_row, me_col)

    def arrivals(q):
        for e in range(1, pairs_n):
            turn(q, from_net(block, a_sems, e, q))

    def handed(q):
        for e in range(pairs_n):
            turn(q, from_partner(block, a_sems, e, q))

    for t in range(1, rows_n):
        q = row_at(t)
        z_copy(q, 1).wait_recv()
        z_send(q)
        ref = block(q, me_col)
        forward(ref, ref, a_sems, 0, q)
        turn(q, me_col)
        arrivals(row_at(t - 1))
        if t > 1:
            handed(row_at(t - 2))

    @pl.when(parity == 1)
    def _():
        @pl.when(me_row != my_pair)
        def _():
            ze_copy(1).wait_recv()
            relay(my_pair, lambda sign: ze_copy(sign).start())
        forward(extra, extra, a_sems, 0, rows_n)
    arrivals(row_at(rows_n - 1))
    if rows_n > 1:
        handed(row_at(rows_n - 2))

    @pl.when(parity == 1)
    def _():
        for e in range(1, pairs_n):
            from_net(block, a_sems, e, rows_n)
    handed(row_at(rows_n - 1))

    @pl.when(parity == 0)
    def _():
        for e in range(pairs_n):
            from_partner(block, a_sems, e, rows_n)

    potential = shift[0]
    order = orders[solver]
    biggest = jnp.zeros((TILE, 1), F32)
    on_diag = eye_block(TILE, TILE, 0)
    for i in range(MAXT):
        ti = lists[solver, i]
        total = jnp.zeros((TILE, TILE), F32)
        for j in range(MAXT):
            tj = lists[solver, j]
            both = hful[tj // TPC, ti]
            w = jnp.where(lax.rem(tj, TPC) == 1, both[:, TILE:], both[:, :TILE])
            w = jnp.where((i < order) & (j < order), w, jnp.zeros_like(w))
            v = w.astype(F32)
            if i == j:
                move = jnp.where(i < order, potential, 0.0)
                v = v - jnp.where(on_diag, move, 0.0)
                w = v.astype(BF)
            xa[i * TILE:(i + 1) * TILE, j * TILE:(j + 1) * TILE] = w
            total = total + v * v
        biggest = jnp.maximum(biggest, jnp.sum(total, axis=1, keepdims=True))
    top = jnp.max(biggest, axis=0, keepdims=True)
    scale = jnp.abs(potential) + 2.0 * jnp.sqrt(top + 1e-06)
    inverse = 1.0 / scale
    lead = 1.5 * inverse
    tail = 0.5 * inverse * inverse * inverse

    def plain(prod, n):
        return prod.astype(BF)

    def upper(ref, n):
        return ref[0:(n + 1) * HALF, n * HALF:(n + 1) * HALF].astype(F32)

    symmetric(xa, xa, fb, plain)
    symmetric(xa, fb, xb, lambda prod, n: (lead * upper(xa, n) - tail * prod).astype(BF))
    symmetric(xb, xb, fb, plain)
    symmetric(xb, fb, xa, lambda prod, n: (1.5 * upper(xb, n) - 0.5 * prod).astype(BF))

    offset = pl.multiple_of(lax.rem(solver * width, TILE), width)
    hit = lax.broadcasted_iota(jnp.int32, (width, SPAN), 0) + offset == lax.broadcasted_iota(
        jnp.int32, (width, SPAN), 1)
    part = xa[pl.ds(offset, width), :]
    q = jnp.dot(part, xa[...], preferred_element_type=F32)
    f = (jnp.where(hit, 1.5, 0.0) - 0.5 * q).astype(BF)
    y = jnp.dot(f, xa[...], preferred_element_type=F32)
    dens = (0.5 * (jnp.where(hit, 1.0, 0.0) - y)).astype(BF)
    for i in range(MAXT):
        cent[i] = dens[:, i * TILE:(i + 1) * TILE]

    my_rows = pl.ds(pl.multiple_of(me_row * width, width), width)

    def place(g, carry):
        where = code[solver, g]
        t = cent[jnp.maximum(where, 0) // 2]
        call[g, my_rows, :] = jnp.where(where >= 0, t, jnp.zeros_like(t))
        return carry
    lax.fori_loop(0, groups, place, 0)

    def part(q, p):
        return call.at[pl.ds(p * gpr, gpr), pl.ds(pl.multiple_of(q * width, width), width), :]

    def direct(p):
        return send(part(me_row, p), part(me_row, p), cd_s.at[p], c_r.at[me_row, p], p, me_col)

    def c_copy(q, p, sign):
        return along(part(q, p), (cu_s if sign > 0 else cl_s).at[q, p], c_r.at[q, p], sign)

    def guarded(q, p, do):
        def make(sign):
            @pl.when(p != me_row + sign)
            def _():
                do(c_copy(q, p, sign))
        relay(q, make)

    def c_wait(q, p):
        c_copy(q, p, 1).wait_recv()
        guarded(q, p, lambda copy: copy.start())

    for t in range(1, rows_n):
        direct(row_at(t)).start()
    for e in range(rows_n):
        guarded(me_row, lax.rem(me_row + e, rows_n), lambda copy: copy.start())

    p_sems = (pn_s, pn_r, pp_s, pp_r)

    def strip_of(t, c):
        return pall.at[c, t]

    for t in range(1, rows_n):
        c_wait(row_at(t), me_row)
    for u in range(gpr):
        forward(call.at[me_row * gpr + u], strip_of(u, me_col), p_sems, 0, u)

    def halves(v, s, g, rows, store):
        cd = code[s, g]
        for h in range(TPC):
            ok = (cd >= 0) & (lax.rem(jnp.maximum(cd, 0), 2) == h)
            store(rows, h, jnp.where(ok, v, jnp.zeros_like(v)))

    def spread(src, c, u):
        for q in range(rows_n):
            def store(rows, h, v):
                ptr[pl.ds(pl.multiple_of(c * wide + q * width, width), width),
                    u * HALF + h * TILE:u * HALF + (h + 1) * TILE] = v
            halves(src[q * width:(q + 1) * width, :], c * rows_n + q, me_row * gpr + u, None, store)

    def own_strip(e):
        for u in range(gpr):
            g = lax.rem(me_row + e, rows_n) * gpr + u
            for q in range(rows_n):
                def store(rows, h, v):
                    ptc[g, q * width:(q + 1) * width, h * TILE:(h + 1) * TILE] = v
                halves(call[g, q * width:(q + 1) * width, :], me_col * rows_n + q, g, None, store)

    own_strip(0)
    for u in range(gpr):
        spread(call.at[me_row * gpr + u], me_col, u)
        dens_out[u * HALF:(u + 1) * HALF, :] = ptc[me_row * gpr + u].T

    def strips(k):
        if k == 0:
            for u in range(gpr):
                for e in range(1, pairs_n):
                    c = from_net(strip_of, p_sems, e, u)
                    spread(pall.at[c, u], c, u)
        if k == rows_n - 2:
            for u in range(gpr):
                for e in range(pairs_n):
                    c = from_partner(strip_of, p_sems, e, u)
                    spread(pall.at[c, u], c, u)

    def strip_product(e):
        p = lax.rem(me_row + e, rows_n)

        def some(h, carry):
            cols = pl.ds(pl.multiple_of(h * HALF, HALF), HALF)
            total = jnp.zeros((wide, HALF), F32) if e == 0 else acc[:, cols]
            for u in range(gpr):
                g = p * gpr + u
                total = total + jnp.dot(
                    ptc[g], hful[h, strip_rows(g)].reshape(HALF, HALF), preferred_element_type=F32)
            if e == rows_n - 1:
                hpt[:, cols] = total.astype(BF)
            else:
                acc[:, cols] = total
            return carry
        lax.fori_loop(0, groups, some, 0)

    strip_product(0)
    for e in range(1, rows_n):
        for t in range(1, rows_n):
            c_wait(row_at(t), lax.rem(me_row + e, rows_n))
        own_strip(e)
        strip_product(e)
        if e < rows_n - 1:
            strips(e - 1)
    strips(rows_n - 2)
    for u in range(gpr):
        php_out[u * HALF:(u + 1) * HALF, :] = jnp.dot(
            hpt[...], ptr[:, u * HALF:(u + 1) * HALF], preferred_element_type=F32).T

    for t in range(rows_n):
        drain(own, a_sems, t)
        relay(row_at(t), lambda sign: z_copy(row_at(t), sign).wait_send())

    @pl.when(parity == 1)
    def _():
        drain(own, a_sems, rows_n)
        relay(my_pair, lambda sign: ze_copy(sign).wait_send())
    for u in range(gpr):
        drain(strip_of(u, me_col), p_sems, u)
    for t in range(rows_n):
        if t:
            direct(row_at(t)).wait_send()
        for p in range(rows_n):
            guarded(row_at(t), p, lambda copy: copy.wait_send())


def per_device(hamiltonian, pattern, tile_lists, orders, shift):
    rows_n = lax.axis_size("row")
    cols_n = lax.axis_size("col")
    high, wide = hamiltonian.shape
    gpr = high // HALF
    groups = rows_n * gpr
    width = wide // rows_n
    pairs_n = cols_n // 2
    steps = jnp.arange(MAXT, dtype=jnp.int32)
    g = jnp.arange(groups, dtype=jnp.int32)
    hit = (tile_lists[:, None, :] // TPC == g[None, :, None]) & (
        steps[None, None, :] < orders[:, None, None])
    code = jnp.max(
        jnp.where(hit, steps[None, None, :] * TPC + tile_lists[:, None, :] % TPC, -1), axis=2)
    dma = pltpu.SemaphoreType.DMA
    smem = pl.BlockSpec(memory_space=pltpu.SMEM)
    vmem = pl.BlockSpec(memory_space=pltpu.VMEM)
    order = rows_n * high
    return pl.pallas_call(
        functools.partial(kernel, rows_n, cols_n),
        out_shape=(
            jax.ShapeDtypeStruct((high, wide), BF),
            jax.ShapeDtypeStruct((high, wide), F32),
        ),
        in_specs=[smem] * 5 + [vmem],
        out_specs=(vmem, vmem),
        scratch_shapes=[
            pltpu.VMEM((cols_n, order // TILE, TILE, wide), BF),
            pltpu.VMEM((SPAN, SPAN), BF),
            pltpu.VMEM((SPAN, SPAN), BF),
            pltpu.VMEM((SPAN, SPAN), BF),
            pltpu.VMEM((MAXT, width, TILE), BF),
            pltpu.VMEM((groups, wide, TILE), BF),
            pltpu.VMEM((cols_n, gpr, wide, TILE), BF),
            pltpu.VMEM((groups, wide, HALF), BF),
            pltpu.VMEM((order, high), BF),
            pltpu.VMEM((wide, order), F32),
            pltpu.VMEM((wide, order), BF),
            *[dma((rows_n,))] * 3,
            dma((2,)), dma,
            *[dma((pairs_n, rows_n + 1))] * 4,
            dma((rows_n,)),
            *[dma((rows_n, rows_n))] * 3,
            *[dma((pairs_n, gpr))] * 4,
        ],
        compiler_params=pltpu.CompilerParams(
            collective_id=0, has_side_effects=True, vmem_limit_bytes=60000000),
    )(code, tile_lists, orders, pattern, shift, hamiltonian)


def solution(mesh):
    in_specs = (P("row", "col"), P(), P(), P(), P())
    out_specs = (P("row", "col"), P("row", "col"))
    return jax.shard_map(
        per_device, mesh=mesh, in_specs=in_specs, out_specs=out_specs, check_vma=False
    )
```

```python
import functools

import jax
import jax.numpy as jnp
from jax import lax
from jax.experimental import pallas as pl
from jax.experimental.pallas import tpu as pltpu
from jax.sharding import PartitionSpec as P

TILE = 128
TPC = 2
MAXT = 8
BF = jnp.bfloat16
F32 = jnp.float32
MESH = pl.DeviceIdType.MESH
SPAN = MAXT * TILE
HALF = TPC * TILE


def eye_block(rows, cols, shift):
    r = lax.broadcasted_iota(jnp.int32, (rows, cols), 0)
    c = lax.broadcasted_iota(jnp.int32, (rows, cols), 1)
    return r == c + shift


def symmetric(left, right, out, finish):
    for n in range(SPAN // HALF):
        cols = slice(n * HALF, (n + 1) * HALF)
        prod = jnp.dot(left[0:(n + 1) * HALF, :], right[:, cols], preferred_element_type=F32)
        done = finish(prod, n)
        out[0:(n + 1) * HALF, cols] = done
        if n:
            out[cols, 0:n * HALF] = done[0:n * HALF, :].T


def kernel(
    rows_n, cols_n, code, lists, orders, pattern, shift, ham,
    dens_out, php_out,
    hful, xa, xb, fb, cent, call, pall, ptc, ptr, acc, hpt,
    zu_s, zd_s, z_r, an_s, an_r, ap_s, ap_r, c_s, c_r,
    pn_s, pn_r, pp_s, pp_r,
):
    me_row = lax.axis_index("row")
    me_col = lax.axis_index("col")
    high, wide = ham.shape
    gpr = high // HALF
    groups = rows_n * gpr
    width = wide // rows_n
    pairs_n = cols_n // 2
    bits = pairs_n.bit_length() - 1
    my_pair = me_col // 2
    parity = lax.rem(me_col, 2)
    partner = my_pair * 2 + 1 - parity
    solver = me_col * rows_n + me_row

    def send(src, dst, ss, rs, row, col):
        return pltpu.make_async_remote_copy(
            src_ref=src, dst_ref=dst, send_sem=ss, recv_sem=rs,
            device_id=(row, col), device_id_type=MESH,
        )

    barrier = pltpu.get_barrier_semaphore()
    for d in range(1, rows_n):
        pl.semaphore_signal(
            barrier, inc=1, device_id=(lax.rem(me_row + d, rows_n), me_col), device_id_type=MESH)
    for d in range(1, cols_n):
        pl.semaphore_signal(
            barrier, inc=1, device_id=(me_row, lax.rem(me_col + d, cols_n)), device_id_type=MESH)
    pl.semaphore_wait(barrier, rows_n - 1 + cols_n - 1)

    def first(q, c):
        p = c // 2
        par = lax.rem(c, 2)
        return jnp.where(q == p, 0, jnp.where(q < p, par, 1 - par))

    def flip(e, par):
        out = 0
        for j in range(bits):
            b = lax.rem(my_pair // (1 << j), 2)
            c0, c1 = (e >> j) & 1, (e >> (bits - 1 - j)) & 1
            if c0 == c1:
                b = 1 - b if c0 else b
            else:
                t = 1 - par if c0 else par
                b = b + t - 2 * b * t
            out = out + (1 << j) * b
        return out

    def column(e, par):
        return flip(e, par) * 2 + par

    def later(e):
        return [i for i in range(bits) if (1 << i) > e]

    def strip_rows(g):
        return pl.ds(g * TPC, TPC)

    below = jnp.where(me_row < rows_n - 1 - me_row, me_row, rows_n - 1 - me_row)
    rest = jnp.where(me_row < rows_n - 1 - me_row, 1, -1)

    def row_at(t):
        near = me_row + (t + 1) // 2 if t % 2 else me_row - t // 2
        return jnp.where(t <= 2 * below, near, me_row + rest * (t - below))

    def group_of(q, c):
        if q is rows_n:
            return c
        return q * gpr + first(q, c)

    def turn(q, c):
        g = group_of(q, c)

        @pl.when(g != c)
        def _():
            hful[g, strip_rows(c)] = hful[c, strip_rows(g)].reshape(HALF, HALF).T.reshape(
                TPC, TILE, HALF)

    def net(src, dst, ss, rs, e, t, i):
        f = e | (1 << i)
        return send(src, dst, ss.at[f, t], rs.at[f, t], me_row, column(1 << i, parity))

    def pass_on(src, dst, ss, rs, e, t):
        return send(src, dst, ss.at[e, t], rs.at[e, t], me_row, partner)

    def forward(src, dst, sems, e, t):
        ns, nr, ps, pr = sems
        for i in later(e):
            net(src, dst, ns, nr, e, t, i).start()
        pass_on(src, dst, ps, pr, e, t).start()

    def from_net(ref, sems, e, t):
        ns, nr, ps, pr = sems
        top = e.bit_length() - 1
        net(ref, ref, ns, nr, e ^ (1 << top), t, top).wait_recv()
        forward(ref, ref, sems, e, t)

    def from_partner(ref, sems, e, t):
        ns, nr, ps, pr = sems
        pass_on(ref, ref, ps, pr, e, t).wait_recv()

    def drain(ref, sems, t):
        ns, nr, ps, pr = sems
        for e in range(pairs_n):
            for i in later(e):
                net(ref, ref, ns, nr, e, t, i).wait_send()
            pass_on(ref, ref, ps, pr, e, t).wait_send()

    a_sems = (an_s, an_r, ap_s, ap_r)

    def keep_own(half, g):
        for a in range(TPC):
            for b in range(TPC):
                ga = g * TPC + a
                gb = me_col * TPC + b
                keep = (pattern[ga, gb] == 1) | (ga == gb)
                t = ham[pl.ds(pl.multiple_of(half * HALF + a * TILE, TILE), TILE),
                        b * TILE:(b + 1) * TILE]
                hful[me_col, g * TPC + a, :, b * TILE:(b + 1) * TILE] = jnp.where(
                    keep, t, jnp.zeros_like(t))

    my_half = first(me_row, me_col)
    keep_own(my_half, me_row * gpr + my_half)

    def along(ref, ss, rs, sign):
        return send(ref, ref, ss, rs, me_row + sign, me_col)

    def relay(q, make):
        @pl.when((q <= me_row) & (me_row < rows_n - 1))
        def _():
            make(1)

        @pl.when((q >= me_row) & (me_row > 0))
        def _():
            make(-1)

    stream = [(t, h) for t in range(rows_n) for h in range(TPC)]
    late = [(rows_n, h) for h in range(TPC)]
    stream = stream[:-TPC] + late + stream[-TPC:]

    def row_of(t):
        return rows_n if t == rows_n else row_at(t)

    def piece(t, h, c):
        return hful.at[c, group_of(row_of(t), c) * TPC + h]

    def index(t, h):
        return row_of(t) * TPC + h

    def z_copy(t, h, sign):
        k = index(t, h)
        return along(piece(t, h, me_col), (zu_s if sign > 0 else zd_s).at[k], z_r.at[k], sign)

    def origin(t):
        return my_pair if t == rows_n else row_at(t)

    def z_send(t, h):
        relay(origin(t), lambda sign: z_copy(t, h, sign).start())

    for h in range(TPC):
        z_send(0, h)
        ref = piece(0, h, me_col)
        forward(ref, ref, a_sems, 0, index(0, h))

    @pl.when((parity == 1) & (me_row == my_pair))
    def _():
        keep_own(1, me_col)
        for h in range(TPC):
            z_send(rows_n, h)
    turn(me_row, me_col)

    def only_odd(t, par, do):
        if t == rows_n:
            pl.when(par == 1)(do)
        else:
            do()

    def enter(t, h):
        def go():
            if t == rows_n:
                @pl.when(me_row != my_pair)
                def _():
                    z_copy(t, h, 1).wait_recv()
                    z_send(t, h)
            elif t:
                z_copy(t, h, 1).wait_recv()
                z_send(t, h)
            ref = piece(t, h, me_col)
            if t:
                forward(ref, ref, a_sems, 0, index(t, h))
            if 0 < t < rows_n and h == TPC - 1:
                turn(row_at(t), me_col)
        only_odd(t, parity, go)

    def arrive(t, h, some):
        def go():
            for e in some:
                c = column(e, parity)
                from_net(piece(t, h, c), a_sems, e, index(t, h))
                if t < rows_n and h == TPC - 1:
                    turn(row_at(t), c)
        only_odd(t, parity, go)

    def handed(t, h):
        def go():
            for e in range(pairs_n):
                c = column(e, 1 - parity)
                from_partner(piece(t, h, c), a_sems, e, index(t, h))
                if t < rows_n and h == TPC - 1:
                    turn(row_at(t), c)
        only_odd(t, 1 - parity, go)

    by_hops = [[e for e in range(1, pairs_n) if bin(e).count("1") == k] for k in range(1, bits + 1)]
    lags = [(2 * k, by_hops[k - 1]) for k in range(1, bits + 1)]
    for i in range(len(stream) + 2 * bits + 2):
        if i < len(stream):
            enter(*stream[i])
        for lag, some in lags:
            if 0 <= i - lag < len(stream):
                arrive(*stream[i - lag], some)
        if 0 <= i - 2 * bits - 1 < len(stream):
            handed(*stream[i - 2 * bits - 1])

    potential = shift[0]
    order = orders[solver]
    biggest = jnp.zeros((TILE, 1), F32)
    on_diag = eye_block(TILE, TILE, 0)
    for i in range(MAXT):
        ti = lists[solver, i]
        total = jnp.zeros((TILE, TILE), F32)
        for j in range(MAXT):
            tj = lists[solver, j]
            both = hful[tj // TPC, ti]
            w = jnp.where(lax.rem(tj, TPC) == 1, both[:, TILE:], both[:, :TILE])
            w = jnp.where((i < order) & (j < order), w, jnp.zeros_like(w))
            v = w.astype(F32)
            if i == j:
                move = jnp.where(i < order, potential, 0.0)
                v = v - jnp.where(on_diag, move, 0.0)
                w = v.astype(BF)
            xa[i * TILE:(i + 1) * TILE, j * TILE:(j + 1) * TILE] = w
            total = total + v * v
        biggest = jnp.maximum(biggest, jnp.sum(total, axis=1, keepdims=True))
    top = jnp.max(biggest, axis=0, keepdims=True)
    scale = jnp.abs(potential) + 2.0 * jnp.sqrt(top + 1e-06)
    inverse = 1.0 / scale
    lead = 1.5 * inverse
    tail = 0.5 * inverse * inverse * inverse

    def plain(prod, n):
        return prod.astype(BF)

    def upper(ref, n):
        return ref[0:(n + 1) * HALF, n * HALF:(n + 1) * HALF].astype(F32)

    symmetric(xa, xa, fb, plain)
    symmetric(xa, fb, xb, lambda prod, n: (lead * upper(xa, n) - tail * prod).astype(BF))
    symmetric(xb, xb, fb, plain)
    symmetric(xb, fb, xa, lambda prod, n: (1.5 * upper(xb, n) - 0.5 * prod).astype(BF))

    offset = pl.multiple_of(lax.rem(solver * width, TILE), width)
    hit = lax.broadcasted_iota(jnp.int32, (width, SPAN), 0) + offset == lax.broadcasted_iota(
        jnp.int32, (width, SPAN), 1)
    part = xa[pl.ds(offset, width), :]
    q = jnp.dot(part, xa[...], preferred_element_type=F32)
    f = (jnp.where(hit, 1.5, 0.0) - 0.5 * q).astype(BF)
    y = jnp.dot(f, xa[...], preferred_element_type=F32)
    dens = (0.5 * (jnp.where(hit, 1.0, 0.0) - y)).astype(BF)
    for i in range(MAXT):
        cent[i] = dens[:, i * TILE:(i + 1) * TILE]

    my_rows = pl.ds(pl.multiple_of(me_row * width, width), width)

    def place(g, carry):
        where = code[solver, g]
        t = cent[jnp.maximum(where, 0) // 2]
        call[g, my_rows, :] = jnp.where(where >= 0, t, jnp.zeros_like(t))
        return carry
    lax.fori_loop(0, groups, place, 0)

    def part(e, d):
        to = lax.rem(me_row + d, rows_n)
        p = lax.rem(me_row + d + e, rows_n)
        ref = call.at[pl.ds(p * gpr, gpr), my_rows, :]
        return send(ref, ref, c_s.at[e, d], c_r.at[e, d], to, me_col)

    def part_in(e, d):
        q = lax.rem(me_row + rows_n - d, rows_n)
        p = lax.rem(me_row + e, rows_n)
        ref = call.at[pl.ds(p * gpr, gpr), pl.ds(pl.multiple_of(q * width, width), width), :]
        return send(ref, ref, c_s.at[e, d], c_r.at[e, d], lax.rem(me_row + d, rows_n), me_col)

    def parts_out(e):
        if e < rows_n:
            for d in range(1, rows_n):
                part(e, d).start()

    def parts_in(e):
        for d in range(1, rows_n):
            part_in(e, d).wait_recv()
        parts_out(e + 2)

    parts_out(0)
    parts_out(1)

    p_sems = (pn_s, pn_r, pp_s, pp_r)

    parts_in(0)
    for u in range(gpr):
        forward(call.at[me_row * gpr + u], pall.at[me_col, u], p_sems, 0, u)

    def halves(v, s, g, rows, store):
        cd = code[s, g]
        for h in range(TPC):
            ok = (cd >= 0) & (lax.rem(jnp.maximum(cd, 0), 2) == h)
            store(rows, h, jnp.where(ok, v, jnp.zeros_like(v)))

    def spread(src, c, u):
        for q in range(rows_n):
            def store(rows, h, v):
                ptr[pl.ds(pl.multiple_of(c * wide + q * width, width), width),
                    u * HALF + h * TILE:u * HALF + (h + 1) * TILE] = v
            halves(src[q * width:(q + 1) * width, :], c * rows_n + q, me_row * gpr + u, None, store)

    def own_strip(e):
        for u in range(gpr):
            g = lax.rem(me_row + e, rows_n) * gpr + u
            for q in range(rows_n):
                def store(rows, h, v):
                    ptc[g, q * width:(q + 1) * width, h * TILE:(h + 1) * TILE] = v
                halves(call[g, q * width:(q + 1) * width, :], me_col * rows_n + q, g, None, store)

    own_strip(0)
    for u in range(gpr):
        spread(call.at[me_row * gpr + u], me_col, u)
        dens_out[u * HALF:(u + 1) * HALF, :] = ptc[me_row * gpr + u].T

    def strips(some):
        for e in some:
            c = column(e, parity)
            for u in range(gpr):
                from_net(pall.at[c, u], p_sems, e, u)
                spread(pall.at[c, u], c, u)

    def strips_handed():
        for e in range(pairs_n):
            c = column(e, 1 - parity)
            for u in range(gpr):
                from_partner(pall.at[c, u], p_sems, e, u)
                spread(pall.at[c, u], c, u)

    def strip_product(e):
        p = lax.rem(me_row + e, rows_n)

        def some(h, carry):
            cols = pl.ds(pl.multiple_of(h * HALF, HALF), HALF)
            total = jnp.zeros((wide, HALF), F32) if e == 0 else acc[:, cols]
            for u in range(gpr):
                g = p * gpr + u
                total = total + jnp.dot(
                    ptc[g], hful[h, strip_rows(g)].reshape(HALF, HALF), preferred_element_type=F32)
            if e == rows_n - 1:
                hpt[:, cols] = total.astype(BF)
            else:
                acc[:, cols] = total
            return carry
        lax.fori_loop(0, groups, some, 0)

    strip_product(0)
    for e in range(1, rows_n):
        if e <= bits:
            strips(by_hops[e - 1])
        if e == rows_n - 1:
            for k in range(e, bits):
                strips(by_hops[k])
            strips_handed()
        parts_in(e)
        own_strip(e)
        strip_product(e)
    for u in range(gpr):
        php_out[u * HALF:(u + 1) * HALF, :] = jnp.dot(
            hpt[...], ptr[:, u * HALF:(u + 1) * HALF], preferred_element_type=F32).T

    for t, h in stream:
        def go():
            drain(piece(0, h, me_col), a_sems, index(t, h))
            relay(origin(t), lambda sign: z_copy(t, h, sign).wait_send())
        only_odd(t, parity, go)
    for u in range(gpr):
        drain(pall.at[me_col, u], p_sems, u)
    for e in range(rows_n):
        for d in range(1, rows_n):
            part(e, d).wait_send()


def per_device(hamiltonian, pattern, tile_lists, orders, shift):
    rows_n = lax.axis_size("row")
    cols_n = lax.axis_size("col")
    high, wide = hamiltonian.shape
    gpr = high // HALF
    groups = rows_n * gpr
    width = wide // rows_n
    pairs_n = cols_n // 2
    steps = jnp.arange(MAXT, dtype=jnp.int32)
    g = jnp.arange(groups, dtype=jnp.int32)
    hit = (tile_lists[:, None, :] // TPC == g[None, :, None]) & (
        steps[None, None, :] < orders[:, None, None])
    code = jnp.max(
        jnp.where(hit, steps[None, None, :] * TPC + tile_lists[:, None, :] % TPC, -1), axis=2)
    dma = pltpu.SemaphoreType.DMA
    smem = pl.BlockSpec(memory_space=pltpu.SMEM)
    vmem = pl.BlockSpec(memory_space=pltpu.VMEM)
    order = rows_n * high
    return pl.pallas_call(
        functools.partial(kernel, rows_n, cols_n),
        out_shape=(
            jax.ShapeDtypeStruct((high, wide), BF),
            jax.ShapeDtypeStruct((high, wide), F32),
        ),
        in_specs=[smem] * 5 + [vmem],
        out_specs=(vmem, vmem),
        scratch_shapes=[
            pltpu.VMEM((cols_n, order // TILE, TILE, wide), BF),
            pltpu.VMEM((SPAN, SPAN), BF),
            pltpu.VMEM((SPAN, SPAN), BF),
            pltpu.VMEM((SPAN, SPAN), BF),
            pltpu.VMEM((MAXT, width, TILE), BF),
            pltpu.VMEM((groups, wide, TILE), BF),
            pltpu.VMEM((cols_n, gpr, wide, TILE), BF),
            pltpu.VMEM((groups, wide, HALF), BF),
            pltpu.VMEM((order, high), BF),
            pltpu.VMEM((wide, order), F32),
            pltpu.VMEM((wide, order), BF),
            *[dma(((rows_n + 1) * TPC,))] * 3,
            *[dma((pairs_n, (rows_n + 1) * TPC))] * 4,
            *[dma((rows_n, rows_n))] * 2,
            *[dma((pairs_n, gpr))] * 4,
        ],
        compiler_params=pltpu.CompilerParams(
            collective_id=0, has_side_effects=True, vmem_limit_bytes=60000000),
    )(code, tile_lists, orders, pattern, shift, hamiltonian)


def solution(mesh):
    in_specs = (P("row", "col"), P(), P(), P(), P())
    out_specs = (P("row", "col"), P("row", "col"))
    return jax.shard_map(
        per_device, mesh=mesh, in_specs=in_specs, out_specs=out_specs, check_vma=False
    )
```

```python
import functools
import math

import jax
import jax.numpy as jnp
from jax import lax
from jax.experimental import pallas as pl
from jax.experimental.pallas import tpu as pltpu
from jax.sharding import PartitionSpec as P

TILE = 128
TPC = 2
MAXT = 8
BF = jnp.bfloat16
F32 = jnp.float32
MESH = pl.DeviceIdType.MESH
SPAN = MAXT * TILE
HALF = TPC * TILE


def eye_block(rows, cols, shift):
    r = lax.broadcasted_iota(jnp.int32, (rows, cols), 0)
    c = lax.broadcasted_iota(jnp.int32, (rows, cols), 1)
    return r == c + shift


def symmetric(left, right, out, finish):
    for n in range(SPAN // HALF):
        cols = slice(n * HALF, (n + 1) * HALF)
        prod = jnp.dot(left[0:(n + 1) * HALF, :], right[:, cols], preferred_element_type=F32)
        done = finish(prod, n)
        out[0:(n + 1) * HALF, cols] = done
        if n:
            out[cols, 0:n * HALF] = done[0:n * HALF, :].T


def kernel(
    rows_n, cols_n, code, lists, orders, pattern, shift, ham,
    dens_out, php_out,
    hful, xa, xb, fb, cent, call, pall, ptc, ptr, acc, hpt,
    zu_s, zd_s, z_r, sx_s, sx_r, sz_s, sz_r, sp_s, sp_r, an_s, an_r, ap_s, ap_r, c_s, c_r,
    pn_s, pn_r, pp_s, pp_r,
):
    me_row = lax.axis_index("row")
    me_col = lax.axis_index("col")
    high, wide = ham.shape
    gpr = high // HALF
    groups = rows_n * gpr
    width = wide // rows_n
    pairs_n = cols_n // 2
    bits = pairs_n.bit_length() - 1
    my_pair = me_col // 2
    parity = lax.rem(me_col, 2)
    partner = my_pair * 2 + 1 - parity
    solver = me_col * rows_n + me_row

    def send(src, dst, ss, rs, row, col):
        return pltpu.make_async_remote_copy(
            src_ref=src, dst_ref=dst, send_sem=ss, recv_sem=rs,
            device_id=(row, col), device_id_type=MESH,
        )

    barrier = pltpu.get_barrier_semaphore()
    for d in range(1, rows_n):
        pl.semaphore_signal(
            barrier, inc=1, device_id=(lax.rem(me_row + d, rows_n), me_col), device_id_type=MESH)
    for d in range(1, cols_n):
        pl.semaphore_signal(
            barrier, inc=1, device_id=(me_row, lax.rem(me_col + d, cols_n)), device_id_type=MESH)
    pl.semaphore_wait(barrier, rows_n - 1 + cols_n - 1)

    def first(q, c):
        p = c // 2
        par = lax.rem(c, 2)
        return jnp.where(q == p, 0, jnp.where(q < p, par, 1 - par))

    def flip(e, par):
        out = 0
        for j in range(bits):
            b = lax.rem(my_pair // (1 << j), 2)
            c0, c1 = (e >> j) & 1, (e >> (bits - 1 - j)) & 1
            if c0 == c1:
                b = 1 - b if c0 else b
            else:
                t = 1 - par if c0 else par
                b = b + t - 2 * b * t
            out = out + (1 << j) * b
        return out

    def column(e, par):
        return flip(e, par) * 2 + par

    def later(e):
        return [i for i in range(bits) if (1 << i) > e]

    def strip_rows(g):
        return pl.ds(g * TPC, TPC)

    below = jnp.where(me_row < rows_n - 1 - me_row, me_row, rows_n - 1 - me_row)
    rest = jnp.where(me_row < rows_n - 1 - me_row, 1, -1)

    def row_at(t):
        near = me_row + (t + 1) // 2 if t % 2 else me_row - t // 2
        return jnp.where(t <= 2 * below, near, me_row + rest * (t - below))

    def group_of(q, c):
        return q * gpr + first(q, c)

    def turn(q, c):
        g = group_of(q, c)

        @pl.when(g != c)
        def _():
            hful[g, strip_rows(c)] = hful[c, strip_rows(g)].reshape(HALF, HALF).T.reshape(
                TPC, TILE, HALF)

    def net(src, dst, ss, rs, e, t, i):
        f = e | (1 << i)
        return send(src, dst, ss.at[f, t], rs.at[f, t], me_row, column(1 << i, parity))

    def pass_on(src, dst, ss, rs, e, t):
        return send(src, dst, ss.at[e, t], rs.at[e, t], me_row, partner)

    def forward(src, dst, sems, e, t):
        ns, nr, ps, pr = sems
        for i in later(e):
            net(src, dst, ns, nr, e, t, i).start()
        pass_on(src, dst, ps, pr, e, t).start()

    def from_net(ref, sems, e, t):
        ns, nr, ps, pr = sems
        top = e.bit_length() - 1
        net(ref, ref, ns, nr, e ^ (1 << top), t, top).wait_recv()
        forward(ref, ref, sems, e, t)

    def from_partner(ref, sems, e, t):
        ns, nr, ps, pr = sems
        pass_on(ref, ref, ps, pr, e, t).wait_recv()

    def drain(ref, sems, t):
        ns, nr, ps, pr = sems
        for e in range(pairs_n):
            for i in later(e):
                net(ref, ref, ns, nr, e, t, i).wait_send()
            pass_on(ref, ref, ps, pr, e, t).wait_send()

    a_sems = (an_s, an_r, ap_s, ap_r)

    def keep_own(half, g):
        for a in range(TPC):
            for b in range(TPC):
                ga = g * TPC + a
                gb = me_col * TPC + b
                keep = (pattern[ga, gb] == 1) | (ga == gb)
                t = ham[pl.ds(pl.multiple_of(half * HALF + a * TILE, TILE), TILE),
                        b * TILE:(b + 1) * TILE]
                hful[me_col, g * TPC + a, :, b * TILE:(b + 1) * TILE] = jnp.where(
                    keep, t, jnp.zeros_like(t))

    my_half = first(me_row, me_col)
    keep_own(my_half, me_row * gpr + my_half)

    def along(ref, ss, rs, sign):
        return send(ref, ref, ss, rs, me_row + sign, me_col)

    def relay(q, make):
        @pl.when((q <= me_row) & (me_row < rows_n - 1))
        def _():
            make(1)

        @pl.when((q >= me_row) & (me_row > 0))
        def _():
            make(-1)

    stream = [(t, h) for t in range(rows_n) for h in range(TPC)]

    def piece(t, h, c):
        return hful.at[c, group_of(row_at(t), c) * TPC + h]

    def index(t, h):
        return row_at(t) * TPC + h

    def z_copy(t, h, sign):
        k = index(t, h)
        return along(piece(t, h, me_col), (zu_s if sign > 0 else zd_s).at[k], z_r.at[k], sign)

    def z_send(t, h):
        relay(row_at(t), lambda sign: z_copy(t, h, sign).start())

    def second(p):
        c = p * 2 + 1
        return hful.at[c, strip_rows(c)]

    def sx_copy(i):
        return send(second(me_row), second(me_row), sx_s.at[i], sx_r, me_row, column(1 << i, parity))

    def sz_copy(p, sign):
        return along(second(p), sz_s.at[p, (sign + 1) // 2], sz_r.at[p], sign)

    def sp_copy(p):
        return send(second(p), second(p), sp_s.at[p], sp_r.at[p], me_row, partner)

    def at_hop(some, do):
        for e in some:
            @pl.when((parity == 1) & (flip(e, parity) == me_row))
            def _():
                do(e)

    def onward(p):
        relay(p, lambda sign: sz_copy(p, sign).start())
        sp_copy(p).start()

    def second_in_row(e):
        if e:
            sx_copy(0).wait_recv()
        for i in later(e):
            sx_copy(i).start()
        onward(me_row)

    def second_along(t):
        @pl.when(parity == 1)
        def _():
            sz_copy(row_at(t), 1).wait_recv()
            onward(row_at(t))

    for h in range(TPC):
        z_send(0, h)
        ref = piece(0, h, me_col)
        forward(ref, ref, a_sems, 0, index(0, h))

    def start_second(e):
        keep_own(1, me_col)
        second_in_row(e)
    at_hop([0], start_second)
    turn(me_row, me_col)

    def enter(t, h):
        if t:
            z_copy(t, h, 1).wait_recv()
            z_send(t, h)
            ref = piece(t, h, me_col)
            forward(ref, ref, a_sems, 0, index(t, h))
            if h == TPC - 1:
                turn(row_at(t), me_col)

    def arrive(t, h, some):
        for e in some:
            c = column(e, parity)
            from_net(piece(t, h, c), a_sems, e, index(t, h))
            if h == TPC - 1:
                turn(row_at(t), c)

    def handed(t, h):
        for e in range(pairs_n):
            c = column(e, 1 - parity)
            from_partner(piece(t, h, c), a_sems, e, index(t, h))
            if h == TPC - 1:
                turn(row_at(t), c)

    by_hops = [[e for e in range(1, pairs_n) if bin(e).count("1") == k] for k in range(1, bits + 1)]
    lags = [(2 * k, by_hops[k - 1]) for k in range(1, bits + 1)]
    for i in range(len(stream) + 2 * bits + 2):
        if i < len(stream):
            enter(*stream[i])
        for lag, some in lags:
            if 0 <= i - lag < len(stream):
                arrive(*stream[i - lag], some)
        k = i - 3
        if 1 <= k <= bits:
            at_hop(by_hops[k - 1], second_in_row)
        if 1 <= k - bits < rows_n:
            second_along(k - bits)
        if 0 <= i - 2 * bits - 1 < len(stream):
            handed(*stream[i - 2 * bits - 1])
    for t in range(max(1, len(stream) + bits - 1), rows_n):
        second_along(t)

    @pl.when(parity == 0)
    def _():
        for p in range(rows_n):
            sp_copy(p).wait_recv()

    potential = shift[0]
    order = orders[solver]
    biggest = jnp.zeros((TILE, 1), F32)
    on_diag = eye_block(TILE, TILE, 0)
    for i in range(MAXT):
        ti = lists[i, solver]
        total = jnp.zeros((TILE, TILE), F32)
        for j in range(MAXT):
            tj = lists[j, solver]
            both = hful[tj // TPC, ti]
            w = jnp.where(lax.rem(tj, TPC) == 1, both[:, TILE:], both[:, :TILE])
            w = jnp.where((i < order) & (j < order), w, jnp.zeros_like(w))
            v = w.astype(F32)
            if i == j:
                move = jnp.where(i < order, potential, 0.0)
                v = v - jnp.where(on_diag, move, 0.0)
                w = v.astype(BF)
            xa[i * TILE:(i + 1) * TILE, j * TILE:(j + 1) * TILE] = w
            total = total + v * v
        biggest = jnp.maximum(biggest, jnp.sum(total, axis=1, keepdims=True))
    top = jnp.max(biggest, axis=0, keepdims=True)
    scale = jnp.abs(potential) + 2.0 * jnp.sqrt(top + 1e-06)
    inverse = 1.0 / scale
    lead = 1.5 * inverse
    tail = 0.5 * inverse * inverse * inverse

    def plain(prod, n):
        return prod.astype(BF)

    def upper(ref, n):
        return ref[0:(n + 1) * HALF, n * HALF:(n + 1) * HALF].astype(F32)

    symmetric(xa, xa, fb, plain)
    symmetric(xa, fb, xb, lambda prod, n: (lead * upper(xa, n) - tail * prod).astype(BF))
    symmetric(xb, xb, fb, plain)
    symmetric(xb, fb, xa, lambda prod, n: (1.5 * upper(xb, n) - 0.5 * prod).astype(BF))

    offset = pl.multiple_of(lax.rem(solver * width, TILE), width)
    hit = lax.broadcasted_iota(jnp.int32, (width, SPAN), 0) + offset == lax.broadcasted_iota(
        jnp.int32, (width, SPAN), 1)
    part = xa[pl.ds(offset, width), :]
    q = jnp.dot(part, xa[...], preferred_element_type=F32)
    f = (jnp.where(hit, 1.5, 0.0) - 0.5 * q).astype(BF)
    y = jnp.dot(f, xa[...], preferred_element_type=F32)
    dens = (0.5 * (jnp.where(hit, 1.0, 0.0) - y)).astype(BF)
    for i in range(MAXT):
        cent[i] = dens[:, i * TILE:(i + 1) * TILE]

    my_rows = pl.ds(pl.multiple_of(me_row * width, width), width)

    def place(g, carry):
        where = code[g, solver]
        t = cent[jnp.maximum(where, 0) // 2]
        call[g, my_rows, :] = jnp.where(where >= 0, t, jnp.zeros_like(t))
        return carry
    lax.fori_loop(0, groups, place, 0)

    def part(e, d):
        to = lax.rem(me_row + d, rows_n)
        p = lax.rem(me_row + d + e, rows_n)
        ref = call.at[pl.ds(p * gpr, gpr), my_rows, :]
        return send(ref, ref, c_s.at[e, d], c_r.at[e, d], to, me_col)

    def part_in(e, d):
        q = lax.rem(me_row + rows_n - d, rows_n)
        p = lax.rem(me_row + e, rows_n)
        ref = call.at[pl.ds(p * gpr, gpr), pl.ds(pl.multiple_of(q * width, width), width), :]
        return send(ref, ref, c_s.at[e, d], c_r.at[e, d], lax.rem(me_row + d, rows_n), me_col)

    def parts_out(e):
        if e < rows_n:
            for d in range(1, rows_n):
                part(e, d).start()

    def parts_in(e):
        for d in range(1, rows_n):
            part_in(e, d).wait_recv()
        parts_out(e + 2)

    parts_out(0)
    parts_out(1)

    p_sems = (pn_s, pn_r, pp_s, pp_r)

    parts_in(0)
    for u in range(gpr):
        forward(call.at[me_row * gpr + u], pall.at[me_col, u], p_sems, 0, u)

    def halves(v, s, g, rows, store):
        cd = code[g, s]
        for h in range(TPC):
            ok = (cd >= 0) & (lax.rem(jnp.maximum(cd, 0), 2) == h)
            store(rows, h, jnp.where(ok, v, jnp.zeros_like(v)))

    def spread(src, c, u):
        for q in range(rows_n):
            def store(rows, h, v):
                ptr[pl.ds(pl.multiple_of(c * wide + q * width, width), width),
                    u * HALF + h * TILE:u * HALF + (h + 1) * TILE] = v
            halves(src[q * width:(q + 1) * width, :], c * rows_n + q, me_row * gpr + u, None, store)

    def own_strip(e):
        for u in range(gpr):
            g = lax.rem(me_row + e, rows_n) * gpr + u
            for q in range(rows_n):
                def store(rows, h, v):
                    ptc[g, q * width:(q + 1) * width, h * TILE:(h + 1) * TILE] = v
                halves(call[g, q * width:(q + 1) * width, :], me_col * rows_n + q, g, None, store)

    own_strip(0)
    for u in range(gpr):
        spread(call.at[me_row * gpr + u], me_col, u)
        dens_out[u * HALF:(u + 1) * HALF, :] = ptc[me_row * gpr + u].T

    def strips(some):
        for e in some:
            c = column(e, parity)
            for u in range(gpr):
                from_net(pall.at[c, u], p_sems, e, u)
                spread(pall.at[c, u], c, u)

    def strips_handed():
        for e in range(pairs_n):
            c = column(e, 1 - parity)
            for u in range(gpr):
                from_partner(pall.at[c, u], p_sems, e, u)
                spread(pall.at[c, u], c, u)

    def strip_product(e):
        p = lax.rem(me_row + e, rows_n)

        def some(h, carry):
            cols = pl.ds(pl.multiple_of(h * HALF, HALF), HALF)
            total = jnp.zeros((wide, HALF), F32) if e == 0 else acc[:, cols]
            for u in range(gpr):
                g = p * gpr + u
                total = total + jnp.dot(
                    ptc[g], hful[h, strip_rows(g)].reshape(HALF, HALF), preferred_element_type=F32)
            if e == rows_n - 1:
                hpt[:, cols] = total.astype(BF)
            else:
                acc[:, cols] = total
            return carry
        lax.fori_loop(0, groups, some, 0)

    strip_product(0)
    for e in range(1, rows_n):
        if e <= bits:
            strips(by_hops[e - 1])
        if e == rows_n - 1:
            for k in range(e, bits):
                strips(by_hops[k])
            strips_handed()
        parts_in(e)
        own_strip(e)
        strip_product(e)
    for u in range(gpr):
        php_out[u * HALF:(u + 1) * HALF, :] = jnp.dot(
            hpt[...], ptr[:, u * HALF:(u + 1) * HALF], preferred_element_type=F32).T

    for t, h in stream:
        drain(piece(0, h, me_col), a_sems, index(t, h))
        relay(row_at(t), lambda sign: z_copy(t, h, sign).wait_send())

    for e in range(pairs_n):
        def sent(e):
            for i in later(e):
                sx_copy(i).wait_send()
        at_hop([e], sent)

    @pl.when(parity == 1)
    def _():
        for t in range(rows_n):
            relay(row_at(t), lambda sign: sz_copy(row_at(t), sign).wait_send())
            sp_copy(row_at(t)).wait_send()
    for u in range(gpr):
        drain(pall.at[me_col, u], p_sems, u)
    for e in range(rows_n):
        for d in range(1, rows_n):
            part(e, d).wait_send()


def per_device(hamiltonian, pattern, tile_lists, orders, shift):
    rows_n = lax.axis_size("row")
    cols_n = lax.axis_size("col")
    high, wide = hamiltonian.shape
    gpr = high // HALF
    groups = rows_n * gpr
    width = wide // rows_n
    pairs_n = cols_n // 2
    steps = jnp.arange(MAXT, dtype=jnp.int32)
    g = jnp.arange(groups, dtype=jnp.int32)
    lists = tile_lists.T
    hit = (lists[None] // TPC == g[:, None, None]) & (steps[:, None] < orders[None, :])[None]
    code = jnp.max(jnp.where(hit, (steps[:, None] * TPC + lists % TPC)[None], -1), axis=1)
    dma = pltpu.SemaphoreType.DMA
    smem = pl.BlockSpec(memory_space=pltpu.SMEM)
    vmem = pl.BlockSpec(memory_space=pltpu.VMEM)
    order = rows_n * high
    scratch = [
        pltpu.VMEM((cols_n, order // TILE, TILE, wide), BF),
        pltpu.VMEM((SPAN, SPAN), BF),
        pltpu.VMEM((SPAN, SPAN), BF),
        pltpu.VMEM((SPAN, SPAN), BF),
        pltpu.VMEM((MAXT, width, TILE), BF),
        pltpu.VMEM((groups, wide, TILE), BF),
        pltpu.VMEM((cols_n, gpr, wide, TILE), BF),
        pltpu.VMEM((groups, wide, HALF), BF),
        pltpu.VMEM((order, high), BF),
        pltpu.VMEM((wide, order), F32),
        pltpu.VMEM((wide, order), BF),
    ]
    held = sum(math.prod(ref.shape) * jnp.dtype(ref.dtype).itemsize for ref in scratch)
    return pl.pallas_call(
        functools.partial(kernel, rows_n, cols_n),
        out_shape=(
            jax.ShapeDtypeStruct((high, wide), BF),
            jax.ShapeDtypeStruct((high, wide), F32),
        ),
        in_specs=[smem] * 5 + [vmem],
        out_specs=(vmem, vmem),
        scratch_shapes=[
            *scratch,
            *[dma((rows_n * TPC,))] * 3,
            dma((pairs_n,)), dma, dma((rows_n, 2)), *[dma((rows_n,))] * 3,
            *[dma((pairs_n, rows_n * TPC))] * 4,
            *[dma((rows_n, rows_n))] * 2,
            *[dma((pairs_n, gpr))] * 4,
        ],
        compiler_params=pltpu.CompilerParams(
            collective_id=0, has_side_effects=True, vmem_limit_bytes=min(60000000, held + 12000000)),
    )(code, lists, orders, pattern, shift, hamiltonian)


def solution(mesh):
    in_specs = (P("row", "col"), P(), P(), P(), P())
    out_specs = (P("row", "col"), P("row", "col"))
    return jax.shard_map(
        per_device, mesh=mesh, in_specs=in_specs, out_specs=out_specs, check_vma=False
    )
```

```python
import functools

import jax
import jax.numpy as jnp
from jax import lax
from jax.experimental import pallas as pl
from jax.experimental.pallas import tpu as pltpu
from jax.sharding import PartitionSpec as P

TILE = 128
TPC = 2
MAXT = 8
BF = jnp.bfloat16
F32 = jnp.float32
MESH = pl.DeviceIdType.MESH
SPAN = MAXT * TILE
HALF = TPC * TILE


def eye_block(rows, cols, shift):
    r = lax.broadcasted_iota(jnp.int32, (rows, cols), 0)
    c = lax.broadcasted_iota(jnp.int32, (rows, cols), 1)
    return r == c + shift


def symmetric(left, right, out, finish):
    for n in range(SPAN // HALF):
        cols = slice(n * HALF, (n + 1) * HALF)
        prod = jnp.dot(left[0:(n + 1) * HALF, :], right[:, cols], preferred_element_type=F32)
        done = finish(prod, n)
        out[0:(n + 1) * HALF, cols] = done
        if n:
            out[cols, 0:n * HALF] = done[0:n * HALF, :].T


def kernel(
    rows_n, cols_n, lists_hbm, orders_hbm, pattern_hbm, shift_hbm, ham_hbm,
    dens_out, php_out,
    ham, lists, orders, pattern, shift, lists_v, code_v, code, in_s, hful, xa, xb, fb, cent, call, pall, ptc, ptr, acc, hpt,
    zu_s, zd_s, z_r, sx_s, sx_r, sz_s, sz_r, sp_s, sp_r, an_s, an_r, ap_s, ap_r, c_s, c_r,
    pn_s, pn_r, pp_s, pp_r,
):
    me_row = lax.axis_index("row")
    me_col = lax.axis_index("col")
    high, wide = ham.shape
    gpr = high // HALF
    groups = rows_n * gpr
    width = wide // rows_n
    pairs_n = cols_n // 2
    bits = pairs_n.bit_length() - 1
    my_pair = me_col // 2
    parity = lax.rem(me_col, 2)
    partner = my_pair * 2 + 1 - parity
    solver = me_col * rows_n + me_row

    def send(src, dst, ss, rs, row, col):
        return pltpu.make_async_remote_copy(
            src_ref=src, dst_ref=dst, send_sem=ss, recv_sem=rs,
            device_id=(row, col), device_id_type=MESH,
        )

    loads = [pltpu.make_async_copy(src, dst, in_s.at[k]) for k, (src, dst) in enumerate((
        (ham_hbm, ham), (pattern_hbm, pattern), (lists_hbm, lists_v), (lists_hbm, lists),
        (orders_hbm, orders), (shift_hbm, shift)))]
    for load in loads:
        load.start()

    barrier = pltpu.get_barrier_semaphore()
    for d in range(1, rows_n):
        pl.semaphore_signal(
            barrier, inc=1, device_id=(lax.rem(me_row + d, rows_n), me_col), device_id_type=MESH)
    for d in range(1, cols_n):
        pl.semaphore_signal(
            barrier, inc=1, device_id=(me_row, lax.rem(me_col + d, cols_n)), device_id_type=MESH)
    pl.semaphore_wait(barrier, rows_n - 1 + cols_n - 1)

    def first(q, c):
        p = c // 2
        par = lax.rem(c, 2)
        return jnp.where(q == p, 0, jnp.where(q < p, par, 1 - par))

    def flip(e, par):
        out = 0
        for j in range(bits):
            b = lax.rem(my_pair // (1 << j), 2)
            c0, c1 = (e >> j) & 1, (e >> (bits - 1 - j)) & 1
            if c0 == c1:
                b = 1 - b if c0 else b
            else:
                t = 1 - par if c0 else par
                b = b + t - 2 * b * t
            out = out + (1 << j) * b
        return out

    def column(e, par):
        return flip(e, par) * 2 + par

    def later(e):
        return [i for i in range(bits) if (1 << i) > e]

    def strip_rows(g):
        return pl.ds(g * TPC, TPC)

    below = jnp.where(me_row < rows_n - 1 - me_row, me_row, rows_n - 1 - me_row)
    rest = jnp.where(me_row < rows_n - 1 - me_row, 1, -1)

    def row_at(t):
        near = me_row + (t + 1) // 2 if t % 2 else me_row - t // 2
        return jnp.where(t <= 2 * below, near, me_row + rest * (t - below))

    def group_of(q, c):
        return q * gpr + first(q, c)

    def turn(q, c):
        g = group_of(q, c)

        @pl.when(g != c)
        def _():
            hful[g, strip_rows(c)] = hful[c, strip_rows(g)].reshape(HALF, HALF).T.reshape(
                TPC, TILE, HALF)

    def net(src, dst, ss, rs, e, t, i):
        f = e | (1 << i)
        return send(src, dst, ss.at[f, t], rs.at[f, t], me_row, column(1 << i, parity))

    def pass_on(src, dst, ss, rs, e, t):
        return send(src, dst, ss.at[e, t], rs.at[e, t], me_row, partner)

    def forward(src, dst, sems, e, t):
        ns, nr, ps, pr = sems
        for i in later(e):
            net(src, dst, ns, nr, e, t, i).start()
        pass_on(src, dst, ps, pr, e, t).start()

    def from_net(ref, sems, e, t):
        ns, nr, ps, pr = sems
        top = e.bit_length() - 1
        net(ref, ref, ns, nr, e ^ (1 << top), t, top).wait_recv()
        forward(ref, ref, sems, e, t)

    def from_partner(ref, sems, e, t):
        ns, nr, ps, pr = sems
        pass_on(ref, ref, ps, pr, e, t).wait_recv()

    def drain(ref, sems, t):
        ns, nr, ps, pr = sems
        for e in range(pairs_n):
            for i in later(e):
                net(ref, ref, ns, nr, e, t, i).wait_send()
            pass_on(ref, ref, ps, pr, e, t).wait_send()

    a_sems = (an_s, an_r, ap_s, ap_r)

    def keep_own(half, g):
        for a in range(TPC):
            for b in range(TPC):
                ga = g * TPC + a
                gb = me_col * TPC + b
                keep = (pattern[ga, gb] == 1) | (ga == gb)
                t = ham[pl.ds(pl.multiple_of(half * HALF + a * TILE, TILE), TILE),
                        b * TILE:(b + 1) * TILE]
                hful[me_col, g * TPC + a, :, b * TILE:(b + 1) * TILE] = jnp.where(
                    keep, t, jnp.zeros_like(t))

    loads[0].wait()
    loads[1].wait()
    my_half = first(me_row, me_col)
    keep_own(my_half, me_row * gpr + my_half)

    def along(ref, ss, rs, sign):
        return send(ref, ref, ss, rs, me_row + sign, me_col)

    def relay(q, make):
        @pl.when((q <= me_row) & (me_row < rows_n - 1))
        def _():
            make(1)

        @pl.when((q >= me_row) & (me_row > 0))
        def _():
            make(-1)

    stream = [(t, h) for t in range(rows_n) for h in range(TPC)]

    def piece(t, h, c):
        return hful.at[c, group_of(row_at(t), c) * TPC + h]

    def index(t, h):
        return row_at(t) * TPC + h

    def z_copy(t, h, sign):
        k = index(t, h)
        return along(piece(t, h, me_col), (zu_s if sign > 0 else zd_s).at[k], z_r.at[k], sign)

    def z_send(t, h):
        relay(row_at(t), lambda sign: z_copy(t, h, sign).start())

    def second(p):
        c = p * 2 + 1
        return hful.at[c, strip_rows(c)]

    def sx_copy(i):
        return send(second(me_row), second(me_row), sx_s.at[i], sx_r, me_row, column(1 << i, parity))

    def sz_copy(p, sign):
        return along(second(p), sz_s.at[p, (sign + 1) // 2], sz_r.at[p], sign)

    def sp_copy(p):
        return send(second(p), second(p), sp_s.at[p], sp_r.at[p], me_row, partner)

    def at_hop(some, do):
        for e in some:
            @pl.when((parity == 1) & (flip(e, parity) == me_row))
            def _():
                do(e)

    def onward(p):
        relay(p, lambda sign: sz_copy(p, sign).start())
        sp_copy(p).start()

    def second_in_row(e):
        if e:
            sx_copy(0).wait_recv()
        for i in later(e):
            sx_copy(i).start()
        onward(me_row)

    def second_along(t):
        @pl.when(parity == 1)
        def _():
            sz_copy(row_at(t), 1).wait_recv()
            onward(row_at(t))

    for h in range(TPC):
        z_send(0, h)
        ref = piece(0, h, me_col)
        forward(ref, ref, a_sems, 0, index(0, h))

    def start_second(e):
        keep_own(1, me_col)
        second_in_row(e)
    at_hop([0], start_second)
    turn(me_row, me_col)

    for load in loads[2:]:
        load.wait()
    tiles = lists_v[...]
    place_of = lax.broadcasted_iota(jnp.int32, tiles.shape, 0) * TPC + lax.rem(tiles, TPC)
    for g in range(groups):
        code_v[g:g + 1, :] = jnp.max(
            jnp.where(tiles // TPC == g, place_of, -1), axis=0, keepdims=True)
    code_load = pltpu.make_async_copy(code_v, code, in_s.at[len(loads)])
    code_load.start()

    def enter(t, h):
        if t:
            z_copy(t, h, 1).wait_recv()
            z_send(t, h)
            ref = piece(t, h, me_col)
            forward(ref, ref, a_sems, 0, index(t, h))
            if h == TPC - 1:
                turn(row_at(t), me_col)

    def arrive(t, h, some):
        for e in some:
            c = column(e, parity)
            from_net(piece(t, h, c), a_sems, e, index(t, h))
            if h == TPC - 1:
                turn(row_at(t), c)

    def handed(t, h):
        for e in range(pairs_n):
            c = column(e, 1 - parity)
            from_partner(piece(t, h, c), a_sems, e, index(t, h))
            if h == TPC - 1:
                turn(row_at(t), c)

    by_hops = [[e for e in range(1, pairs_n) if bin(e).count("1") == k] for k in range(1, bits + 1)]
    lags = [(2 * k, by_hops[k - 1]) for k in range(1, bits + 1)]
    for i in range(len(stream) + 4 * bits):
        if i < len(stream):
            enter(*stream[i])
        for lag, some in lags:
            if 0 <= i - lag < len(stream):
                arrive(*stream[i - lag], some)
        k = i - 1
        if 1 <= k <= bits:
            at_hop(by_hops[k - 1], second_in_row)
        if 1 <= k - bits < rows_n:
            second_along(k - bits)
        if 0 <= i - 4 * bits < len(stream):
            handed(*stream[i - 4 * bits])

    @pl.when(parity == 0)
    def _():
        for p in range(rows_n):
            sp_copy(p).wait_recv()

    code_load.wait()

    potential = shift[0]
    order = orders[solver]
    biggest = jnp.zeros((TILE, 1), F32)
    on_diag = eye_block(TILE, TILE, 0)
    for i in range(MAXT):
        ti = lists[i, solver]
        total = jnp.zeros((TILE, TILE), F32)
        for j in range(MAXT):
            tj = lists[j, solver]
            both = hful[tj // TPC, ti]
            w = jnp.where(lax.rem(tj, TPC) == 1, both[:, TILE:], both[:, :TILE])
            w = jnp.where((i < order) & (j < order), w, jnp.zeros_like(w))
            v = w.astype(F32)
            if i == j:
                move = jnp.where(i < order, potential, 0.0)
                v = v - jnp.where(on_diag, move, 0.0)
                w = v.astype(BF)
            xa[i * TILE:(i + 1) * TILE, j * TILE:(j + 1) * TILE] = w
            total = total + v * v
        biggest = jnp.maximum(biggest, jnp.sum(total, axis=1, keepdims=True))
    top = jnp.max(biggest, axis=0, keepdims=True)
    scale = jnp.abs(potential) + 2.0 * jnp.sqrt(top + 1e-06)
    inverse = 1.0 / scale
    lead = 1.5 * inverse
    tail = 0.5 * inverse * inverse * inverse

    def plain(prod, n):
        return prod.astype(BF)

    def upper(ref, n):
        return ref[0:(n + 1) * HALF, n * HALF:(n + 1) * HALF].astype(F32)

    symmetric(xa, xa, fb, plain)
    symmetric(xa, fb, xb, lambda prod, n: (lead * upper(xa, n) - tail * prod).astype(BF))
    symmetric(xb, xb, fb, plain)
    symmetric(xb, fb, xa, lambda prod, n: (1.5 * upper(xb, n) - 0.5 * prod).astype(BF))

    offset = pl.multiple_of(lax.rem(solver * width, TILE), width)
    hit = lax.broadcasted_iota(jnp.int32, (width, SPAN), 0) + offset == lax.broadcasted_iota(
        jnp.int32, (width, SPAN), 1)
    part = xa[pl.ds(offset, width), :]
    q = jnp.dot(part, xa[...], preferred_element_type=F32)
    f = (jnp.where(hit, 1.5, 0.0) - 0.5 * q).astype(BF)
    y = jnp.dot(f, xa[...], preferred_element_type=F32)
    dens = (0.5 * (jnp.where(hit, 1.0, 0.0) - y)).astype(BF)
    for i in range(MAXT):
        cent[i] = dens[:, i * TILE:(i + 1) * TILE]

    my_rows = pl.ds(pl.multiple_of(me_row * width, width), width)

    def code_of(g, s):
        cd = code[g, s]
        return jnp.where(jnp.maximum(cd, 0) // TPC < orders[s], cd, -1)

    def place(g, carry):
        where = code_of(g, solver)
        t = cent[jnp.maximum(where, 0) // 2]
        call[g, my_rows, :] = jnp.where(where >= 0, t, jnp.zeros_like(t))
        return carry
    lax.fori_loop(0, groups, place, 0)

    def part(e, d):
        to = lax.rem(me_row + d, rows_n)
        p = lax.rem(me_row + d + e, rows_n)
        ref = call.at[pl.ds(p * gpr, gpr), my_rows, :]
        return send(ref, ref, c_s.at[e, d], c_r.at[e, d], to, me_col)

    def part_in(e, d):
        q = lax.rem(me_row + rows_n - d, rows_n)
        p = lax.rem(me_row + e, rows_n)
        ref = call.at[pl.ds(p * gpr, gpr), pl.ds(pl.multiple_of(q * width, width), width), :]
        return send(ref, ref, c_s.at[e, d], c_r.at[e, d], lax.rem(me_row + d, rows_n), me_col)

    def parts_out(e):
        if e < rows_n:
            for d in range(1, rows_n):
                part(e, d).start()

    def parts_in(e):
        for d in range(1, rows_n):
            part_in(e, d).wait_recv()
        parts_out(e + 2)

    parts_out(0)
    parts_out(1)

    p_sems = (pn_s, pn_r, pp_s, pp_r)

    parts_in(0)
    for u in range(gpr):
        forward(call.at[me_row * gpr + u], pall.at[me_col, u], p_sems, 0, u)

    def halves(v, s, g, rows, store):
        cd = code_of(g, s)
        for h in range(TPC):
            ok = (cd >= 0) & (lax.rem(jnp.maximum(cd, 0), 2) == h)
            store(rows, h, jnp.where(ok, v, jnp.zeros_like(v)))

    def spread(src, c, u):
        for q in range(rows_n):
            def store(rows, h, v):
                ptr[pl.ds(pl.multiple_of(c * wide + q * width, width), width),
                    u * HALF + h * TILE:u * HALF + (h + 1) * TILE] = v
            halves(src[q * width:(q + 1) * width, :], c * rows_n + q, me_row * gpr + u, None, store)

    def own_strip(e):
        for u in range(gpr):
            g = lax.rem(me_row + e, rows_n) * gpr + u
            for q in range(rows_n):
                def store(rows, h, v):
                    ptc[g, q * width:(q + 1) * width, h * TILE:(h + 1) * TILE] = v
                halves(call[g, q * width:(q + 1) * width, :], me_col * rows_n + q, g, None, store)

    own_strip(0)
    for u in range(gpr):
        spread(call.at[me_row * gpr + u], me_col, u)
        dens_out[u * HALF:(u + 1) * HALF, :] = ptc[me_row * gpr + u].T

    def strips(some):
        for e in some:
            c = column(e, parity)
            for u in range(gpr):
                from_net(pall.at[c, u], p_sems, e, u)
                spread(pall.at[c, u], c, u)

    def strips_handed():
        for e in range(pairs_n):
            c = column(e, 1 - parity)
            for u in range(gpr):
                from_partner(pall.at[c, u], p_sems, e, u)
                spread(pall.at[c, u], c, u)

    def strip_product(e):
        p = lax.rem(me_row + e, rows_n)

        def some(h, carry):
            cols = pl.ds(pl.multiple_of(h * HALF, HALF), HALF)
            total = jnp.zeros((wide, HALF), F32) if e == 0 else acc[:, cols]
            for u in range(gpr):
                g = p * gpr + u
                total = total + jnp.dot(
                    ptc[g], hful[h, strip_rows(g)].reshape(HALF, HALF), preferred_element_type=F32)
            if e == rows_n - 1:
                hpt[:, cols] = total.astype(BF)
            else:
                acc[:, cols] = total
            return carry
        lax.fori_loop(0, groups, some, 0)

    strip_product(0)
    for e in range(1, rows_n):
        if e <= bits:
            strips(by_hops[e - 1])
        if e == rows_n - 1:
            for k in range(e, bits):
                strips(by_hops[k])
            strips_handed()
        parts_in(e)
        own_strip(e)
        strip_product(e)
    for u in range(gpr):
        php_out[u * HALF:(u + 1) * HALF, :] = jnp.dot(
            hpt[...], ptr[:, u * HALF:(u + 1) * HALF], preferred_element_type=F32).T

    for t, h in stream:
        drain(piece(0, h, me_col), a_sems, index(t, h))
        relay(row_at(t), lambda sign: z_copy(t, h, sign).wait_send())

    for e in range(pairs_n):
        def sent(e):
            for i in later(e):
                sx_copy(i).wait_send()
        at_hop([e], sent)

    @pl.when(parity == 1)
    def _():
        for t in range(rows_n):
            relay(row_at(t), lambda sign: sz_copy(row_at(t), sign).wait_send())
            sp_copy(row_at(t)).wait_send()
    for u in range(gpr):
        drain(pall.at[me_col, u], p_sems, u)
    for e in range(rows_n):
        for d in range(1, rows_n):
            part(e, d).wait_send()


def per_device(hamiltonian, pattern, tile_lists, orders, shift):
    rows_n = lax.axis_size("row")
    cols_n = lax.axis_size("col")
    high, wide = hamiltonian.shape
    gpr = high // HALF
    groups = rows_n * gpr
    width = wide // rows_n
    pairs_n = cols_n // 2
    solvers = tile_lists.shape[0]
    blocks = pattern.shape[0]
    dma = pltpu.SemaphoreType.DMA
    smem = pltpu.SMEM
    hbm = pl.BlockSpec(memory_space=pltpu.HBM)
    vmem = pl.BlockSpec(memory_space=pltpu.VMEM)
    order = rows_n * high
    scratch = [
        pltpu.VMEM((cols_n, order // TILE, TILE, wide), BF),
        pltpu.VMEM((SPAN, SPAN), BF),
        pltpu.VMEM((SPAN, SPAN), BF),
        pltpu.VMEM((SPAN, SPAN), BF),
        pltpu.VMEM((MAXT, width, TILE), BF),
        pltpu.VMEM((groups, wide, TILE), BF),
        pltpu.VMEM((cols_n, gpr, wide, TILE), BF),
        pltpu.VMEM((groups, wide, HALF), BF),
        pltpu.VMEM((order, high), BF),
        pltpu.VMEM((wide, order), F32),
        pltpu.VMEM((wide, order), BF),
    ]
    return pl.pallas_call(
        functools.partial(kernel, rows_n, cols_n),
        out_shape=(
            jax.ShapeDtypeStruct((high, wide), BF),
            jax.ShapeDtypeStruct((high, wide), F32),
        ),
        in_specs=[hbm] * 5,
        out_specs=(vmem, vmem),
        scratch_shapes=[
            pltpu.VMEM((high, wide), BF),
            smem((MAXT, solvers), jnp.int32),
            smem((solvers,), jnp.int32),
            smem((blocks, blocks), jnp.int32),
            smem((1,), F32),
            pltpu.VMEM((MAXT, solvers), jnp.int32),
            pltpu.VMEM((groups, solvers), jnp.int32),
            smem((groups, solvers), jnp.int32),
            dma((7,)),
            *scratch,
            *[dma((rows_n * TPC,))] * 3,
            dma((pairs_n,)), dma, dma((rows_n, 2)), *[dma((rows_n,))] * 3,
            *[dma((pairs_n, rows_n * TPC))] * 4,
            *[dma((rows_n, rows_n))] * 2,
            *[dma((pairs_n, gpr))] * 4,
        ],
        compiler_params=pltpu.CompilerParams(
            collective_id=0, has_side_effects=True, vmem_limit_bytes=60000000),
    )(tile_lists.T, orders, pattern, shift, hamiltonian)


def solution(mesh):
    in_specs = (P("row", "col"), P(), P(), P(), P())
    out_specs = (P("row", "col"), P("row", "col"))
    return jax.shard_map(
        per_device, mesh=mesh, in_specs=in_specs, out_specs=out_specs, check_vma=False
    )
```

```python
import functools

import jax
import jax.numpy as jnp
from jax import lax
from jax.experimental import pallas as pl
from jax.experimental.pallas import tpu as pltpu
from jax.sharding import PartitionSpec as P

TILE = 128
TPC = 2
MAXT = 8
BF = jnp.bfloat16
F32 = jnp.float32
MESH = pl.DeviceIdType.MESH
SPAN = MAXT * TILE
HALF = TPC * TILE
PIECES = 2


def eye_block(rows, cols, shift):
    r = lax.broadcasted_iota(jnp.int32, (rows, cols), 0)
    c = lax.broadcasted_iota(jnp.int32, (rows, cols), 1)
    return r == c + shift


def symmetric(left, right, out, finish):
    for n in range(SPAN // HALF):
        cols = slice(n * HALF, (n + 1) * HALF)
        prod = jnp.dot(left[0:(n + 1) * HALF, :], right[:, cols], preferred_element_type=F32)
        done = finish(prod, n)
        out[0:(n + 1) * HALF, cols] = done
        if n:
            out[cols, 0:n * HALF] = done[0:n * HALF, :].T


def kernel(
    rows_n, cols_n, lists_hbm, orders_hbm, pattern_hbm, shift_hbm, ham_hbm,
    dens_out, php_out,
    ham, lists, orders, pattern, shift, lists_v, code_v, code, in_s, dens_v, php_v, out_s, hful, xa, xb, fb, cent, call, pall, ptc, ptr, acc, hpt,
    zu_s, zd_s, z_r, sx_s, sx_r, sz_s, sz_r, sp_s, sp_r, an_s, an_r, ap_s, ap_r, c_s, c_r,
    pn_s, pn_r, pp_s, pp_r,
):
    me_row = lax.axis_index("row")
    me_col = lax.axis_index("col")
    high, wide = ham.shape
    gpr = high // HALF
    groups = rows_n * gpr
    width = wide // rows_n
    pairs_n = cols_n // 2
    bits = pairs_n.bit_length() - 1
    my_pair = me_col // 2
    parity = lax.rem(me_col, 2)
    partner = my_pair * 2 + 1 - parity
    solver = me_col * rows_n + me_row

    def send(src, dst, ss, rs, row, col):
        return pltpu.make_async_remote_copy(
            src_ref=src, dst_ref=dst, send_sem=ss, recv_sem=rs,
            device_id=(row, col), device_id_type=MESH,
        )

    loads = [pltpu.make_async_copy(src, dst, in_s.at[k]) for k, (src, dst) in enumerate((
        (ham_hbm, ham), (pattern_hbm, pattern), (lists_hbm, lists_v), (lists_hbm, lists),
        (orders_hbm, orders), (shift_hbm, shift)))]
    for load in loads:
        load.start()

    barrier = pltpu.get_barrier_semaphore()
    for d in range(1, rows_n):
        pl.semaphore_signal(
            barrier, inc=1, device_id=(lax.rem(me_row + d, rows_n), me_col), device_id_type=MESH)
    for d in range(1, cols_n):
        pl.semaphore_signal(
            barrier, inc=1, device_id=(me_row, lax.rem(me_col + d, cols_n)), device_id_type=MESH)
    pl.semaphore_wait(barrier, rows_n - 1 + cols_n - 1)

    def first(q, c):
        p = c // 2
        par = lax.rem(c, 2)
        return jnp.where(q == p, 0, jnp.where(q < p, par, 1 - par))

    def flip(e, par):
        out = 0
        for j in range(bits):
            b = lax.rem(my_pair // (1 << j), 2)
            c0, c1 = (e >> j) & 1, (e >> (bits - 1 - j)) & 1
            if c0 == c1:
                b = 1 - b if c0 else b
            else:
                t = 1 - par if c0 else par
                b = b + t - 2 * b * t
            out = out + (1 << j) * b
        return out

    def column(e, par):
        return flip(e, par) * 2 + par

    def later(e):
        return [i for i in range(bits) if (1 << i) > e]

    def strip_rows(g):
        return pl.ds(g * TPC, TPC)

    below = jnp.where(me_row < rows_n - 1 - me_row, me_row, rows_n - 1 - me_row)
    rest = jnp.where(me_row < rows_n - 1 - me_row, 1, -1)

    def row_at(t):
        near = me_row + (t + 1) // 2 if t % 2 else me_row - t // 2
        return jnp.where(t <= 2 * below, near, me_row + rest * (t - below))

    def group_of(q, c):
        return q * gpr + first(q, c)

    def turn(q, c):
        g = group_of(q, c)

        @pl.when(g != c)
        def _():
            hful[g, strip_rows(c)] = hful[c, strip_rows(g)].reshape(HALF, HALF).T.reshape(
                TPC, TILE, HALF)

    def net(src, dst, ss, rs, e, t, i):
        f = e | (1 << i)
        return send(src, dst, ss.at[f, t], rs.at[f, t], me_row, column(1 << i, parity))

    def pass_on(src, dst, ss, rs, e, t):
        return send(src, dst, ss.at[e, t], rs.at[e, t], me_row, partner)

    def forward(src, dst, sems, e, t):
        ns, nr, ps, pr = sems
        for i in later(e):
            net(src, dst, ns, nr, e, t, i).start()
        pass_on(src, dst, ps, pr, e, t).start()

    def from_net(ref, sems, e, t):
        ns, nr, ps, pr = sems
        top = e.bit_length() - 1
        net(ref, ref, ns, nr, e ^ (1 << top), t, top).wait_recv()
        forward(ref, ref, sems, e, t)

    def from_partner(ref, sems, e, t):
        ns, nr, ps, pr = sems
        pass_on(ref, ref, ps, pr, e, t).wait_recv()

    def drain(ref, sems, t):
        ns, nr, ps, pr = sems
        for e in range(pairs_n):
            for i in later(e):
                net(ref, ref, ns, nr, e, t, i).wait_send()
            pass_on(ref, ref, ps, pr, e, t).wait_send()

    a_sems = (an_s, an_r, ap_s, ap_r)

    def keep_own(half, g):
        for a in range(TPC):
            for b in range(TPC):
                ga = g * TPC + a
                gb = me_col * TPC + b
                keep = (pattern[ga, gb] == 1) | (ga == gb)
                t = ham[pl.ds(pl.multiple_of(half * HALF + a * TILE, TILE), TILE),
                        b * TILE:(b + 1) * TILE]
                hful[me_col, g * TPC + a, :, b * TILE:(b + 1) * TILE] = jnp.where(
                    keep, t, jnp.zeros_like(t))

    loads[0].wait()
    loads[1].wait()
    my_half = first(me_row, me_col)
    keep_own(my_half, me_row * gpr + my_half)

    def along(ref, ss, rs, sign):
        return send(ref, ref, ss, rs, me_row + sign, me_col)

    def relay(q, make):
        @pl.when((q <= me_row) & (me_row < rows_n - 1))
        def _():
            make(1)

        @pl.when((q >= me_row) & (me_row > 0))
        def _():
            make(-1)

    stream = [(t, h) for t in range(rows_n) for h in range(TPC)]

    def piece(t, h, c):
        return hful.at[c, group_of(row_at(t), c) * TPC + h]

    def index(t, h):
        return row_at(t) * TPC + h

    def z_copy(t, h, sign):
        k = index(t, h)
        return along(piece(t, h, me_col), (zu_s if sign > 0 else zd_s).at[k], z_r.at[k], sign)

    def z_send(t, h):
        relay(row_at(t), lambda sign: z_copy(t, h, sign).start())

    def second(p):
        c = p * 2 + 1
        return hful.at[c, strip_rows(c)]

    def sx_copy(i):
        return send(second(me_row), second(me_row), sx_s.at[i], sx_r, me_row, column(1 << i, parity))

    def sz_copy(p, sign):
        return along(second(p), sz_s.at[p, (sign + 1) // 2], sz_r.at[p], sign)

    def sp_copy(p):
        return send(second(p), second(p), sp_s.at[p], sp_r.at[p], me_row, partner)

    def at_hop(some, do):
        for e in some:
            @pl.when((parity == 1) & (flip(e, parity) == me_row))
            def _():
                do(e)

    def onward(p):
        relay(p, lambda sign: sz_copy(p, sign).start())
        sp_copy(p).start()

    def second_in_row(e):
        if e:
            sx_copy(0).wait_recv()
        for i in later(e):
            sx_copy(i).start()
        onward(me_row)

    def second_along(t):
        @pl.when(parity == 1)
        def _():
            sz_copy(row_at(t), 1).wait_recv()
            onward(row_at(t))

    for h in range(TPC):
        z_send(0, h)
        ref = piece(0, h, me_col)
        forward(ref, ref, a_sems, 0, index(0, h))

    def start_second(e):
        keep_own(1, me_col)
        second_in_row(e)
    at_hop([0], start_second)
    turn(me_row, me_col)

    for load in loads[2:]:
        load.wait()
    tiles = lists_v[...]
    place_of = lax.broadcasted_iota(jnp.int32, tiles.shape, 0) * TPC + lax.rem(tiles, TPC)
    for g in range(groups):
        code_v[g:g + 1, :] = jnp.max(
            jnp.where(tiles // TPC == g, place_of, -1), axis=0, keepdims=True)
    code_load = pltpu.make_async_copy(code_v, code, in_s.at[len(loads)])
    code_load.start()

    def enter(t, h):
        if t:
            z_copy(t, h, 1).wait_recv()
            z_send(t, h)
            ref = piece(t, h, me_col)
            forward(ref, ref, a_sems, 0, index(t, h))
            if h == TPC - 1:
                turn(row_at(t), me_col)

    def arrive(t, h, some):
        for e in some:
            c = column(e, parity)
            from_net(piece(t, h, c), a_sems, e, index(t, h))
            if h == TPC - 1:
                turn(row_at(t), c)

    def handed(t, h):
        for e in range(pairs_n):
            c = column(e, 1 - parity)
            from_partner(piece(t, h, c), a_sems, e, index(t, h))
            if h == TPC - 1:
                turn(row_at(t), c)

    by_hops = [[e for e in range(1, pairs_n) if bin(e).count("1") == k] for k in range(1, bits + 1)]
    lags = [(2 * k, by_hops[k - 1]) for k in range(1, bits + 1)]
    for i in range(len(stream) + 4 * bits):
        if i < len(stream):
            enter(*stream[i])
        for lag, some in lags:
            if 0 <= i - lag < len(stream):
                arrive(*stream[i - lag], some)
        k = i - 1
        if 1 <= k <= bits:
            at_hop(by_hops[k - 1], second_in_row)
        if 1 <= k - bits < rows_n:
            second_along(k - bits)
        if 0 <= i - 4 * bits < len(stream):
            handed(*stream[i - 4 * bits])

    @pl.when(parity == 0)
    def _():
        for p in range(rows_n):
            sp_copy(p).wait_recv()

    code_load.wait()

    potential = shift[0]
    order = orders[solver]
    biggest = jnp.zeros((TILE, 1), F32)
    on_diag = eye_block(TILE, TILE, 0)
    for i in range(MAXT):
        ti = lists[i, solver]
        total = jnp.zeros((TILE, TILE), F32)
        for j in range(MAXT):
            tj = lists[j, solver]
            both = hful[tj // TPC, ti]
            w = jnp.where(lax.rem(tj, TPC) == 1, both[:, TILE:], both[:, :TILE])
            w = jnp.where((i < order) & (j < order), w, jnp.zeros_like(w))
            v = w.astype(F32)
            if i == j:
                move = jnp.where(i < order, potential, 0.0)
                v = v - jnp.where(on_diag, move, 0.0)
                w = v.astype(BF)
            xa[i * TILE:(i + 1) * TILE, j * TILE:(j + 1) * TILE] = w
            total = total + v * v
        biggest = jnp.maximum(biggest, jnp.sum(total, axis=1, keepdims=True))
    top = jnp.max(biggest, axis=0, keepdims=True)
    scale = jnp.abs(potential) + 2.0 * jnp.sqrt(top + 1e-06)
    inverse = 1.0 / scale
    lead = 1.5 * inverse
    tail = 0.5 * inverse * inverse * inverse

    def plain(prod, n):
        return prod.astype(BF)

    def upper(ref, n):
        return ref[0:(n + 1) * HALF, n * HALF:(n + 1) * HALF].astype(F32)

    symmetric(xa, xa, fb, plain)
    symmetric(xa, fb, xb, lambda prod, n: (lead * upper(xa, n) - tail * prod).astype(BF))
    symmetric(xb, xb, fb, plain)
    symmetric(xb, fb, xa, lambda prod, n: (1.5 * upper(xb, n) - 0.5 * prod).astype(BF))

    offset = pl.multiple_of(lax.rem(solver * width, TILE), width)
    hit = lax.broadcasted_iota(jnp.int32, (width, SPAN), 0) + offset == lax.broadcasted_iota(
        jnp.int32, (width, SPAN), 1)
    part = xa[pl.ds(offset, width), :]
    q = jnp.dot(part, xa[...], preferred_element_type=F32)
    f = (jnp.where(hit, 1.5, 0.0) - 0.5 * q).astype(BF)
    y = jnp.dot(f, xa[...], preferred_element_type=F32)
    dens = (0.5 * (jnp.where(hit, 1.0, 0.0) - y)).astype(BF)
    for i in range(MAXT):
        cent[i] = dens[:, i * TILE:(i + 1) * TILE]

    my_rows = pl.ds(pl.multiple_of(me_row * width, width), width)

    def code_of(g, s):
        cd = code[g, s]
        return jnp.where(jnp.maximum(cd, 0) // TPC < orders[s], cd, -1)

    def place(g, carry):
        where = code_of(g, solver)
        t = cent[jnp.maximum(where, 0) // 2]
        call[g, my_rows, :] = jnp.where(where >= 0, t, jnp.zeros_like(t))
        return carry
    lax.fori_loop(0, groups, place, 0)

    def part(e, d):
        to = lax.rem(me_row + d, rows_n)
        p = lax.rem(me_row + d + e, rows_n)
        ref = call.at[pl.ds(p * gpr, gpr), my_rows, :]
        return send(ref, ref, c_s.at[e, d], c_r.at[e, d], to, me_col)

    def part_in(e, d):
        q = lax.rem(me_row + rows_n - d, rows_n)
        p = lax.rem(me_row + e, rows_n)
        ref = call.at[pl.ds(p * gpr, gpr), pl.ds(pl.multiple_of(q * width, width), width), :]
        return send(ref, ref, c_s.at[e, d], c_r.at[e, d], lax.rem(me_row + d, rows_n), me_col)

    def parts_out(e):
        if e < rows_n:
            for d in range(1, rows_n):
                part(e, d).start()

    def parts_in(e):
        for d in range(1, rows_n):
            part_in(e, d).wait_recv()
        parts_out(e + 2)

    parts_out(0)
    parts_out(1)

    p_sems = (pn_s, pn_r, pp_s, pp_r)

    parts_in(0)
    for u in range(gpr):
        forward(call.at[me_row * gpr + u], pall.at[me_col, u], p_sems, 0, u)

    def halves(v, s, g, rows, store):
        cd = code_of(g, s)
        for h in range(TPC):
            ok = (cd >= 0) & (lax.rem(jnp.maximum(cd, 0), 2) == h)
            store(rows, h, jnp.where(ok, v, jnp.zeros_like(v)))

    def spread(src, c, u):
        for q in range(rows_n):
            def store(rows, h, v):
                ptr[pl.ds(pl.multiple_of(c * wide + q * width, width), width),
                    u * HALF + h * TILE:u * HALF + (h + 1) * TILE] = v
            halves(src[q * width:(q + 1) * width, :], c * rows_n + q, me_row * gpr + u, None, store)

    def own_strip(e):
        for u in range(gpr):
            g = lax.rem(me_row + e, rows_n) * gpr + u
            for q in range(rows_n):
                def store(rows, h, v):
                    ptc[g, q * width:(q + 1) * width, h * TILE:(h + 1) * TILE] = v
                halves(call[g, q * width:(q + 1) * width, :], me_col * rows_n + q, g, None, store)

    own_strip(0)
    for u in range(gpr):
        spread(call.at[me_row * gpr + u], me_col, u)
        dens_v[u * HALF:(u + 1) * HALF, :] = ptc[me_row * gpr + u].T

    dens_load = pltpu.make_async_copy(dens_v, dens_out, out_s.at[gpr])
    dens_load.start()

    def strips(some):
        for e in some:
            c = column(e, parity)
            for u in range(gpr):
                from_net(pall.at[c, u], p_sems, e, u)
                spread(pall.at[c, u], c, u)

    def strips_handed():
        for e in range(pairs_n):
            c = column(e, 1 - parity)
            for u in range(gpr):
                from_partner(pall.at[c, u], p_sems, e, u)
                spread(pall.at[c, u], c, u)

    def strip_product(e):
        p = lax.rem(me_row + e, rows_n)

        def some(h, carry):
            cols = pl.ds(pl.multiple_of(h * HALF, HALF), HALF)
            total = jnp.zeros((wide, HALF), F32) if e == 0 else acc[:, cols]
            for u in range(gpr):
                g = p * gpr + u
                total = total + jnp.dot(
                    ptc[g], hful[h, strip_rows(g)].reshape(HALF, HALF), preferred_element_type=F32)
            if e == rows_n - 1:
                hpt[:, cols] = total.astype(BF)
            else:
                acc[:, cols] = total
            return carry
        lax.fori_loop(0, groups, some, 0)

    def settle_blocks():
        for t, h in stream:
            drain(piece(0, h, me_col), a_sems, index(t, h))
            relay(row_at(t), lambda sign: z_copy(t, h, sign).wait_send())

        for e in range(pairs_n):
            def sent(e):
                for i in later(e):
                    sx_copy(i).wait_send()
            at_hop([e], sent)

        @pl.when(parity == 1)
        def _():
            for t in range(rows_n):
                relay(row_at(t), lambda sign: sz_copy(row_at(t), sign).wait_send())
                sp_copy(row_at(t)).wait_send()

    def settle_parts(e):
        for d in range(1, rows_n):
            part(e, d).wait_send()

    strip_product(0)
    settle_blocks()
    for e in range(1, rows_n):
        if e <= bits:
            strips(by_hops[e - 1])
        if e == rows_n - 1:
            for k in range(e, bits):
                strips(by_hops[k])
            strips_handed()
            for u in range(gpr):
                drain(pall.at[me_col, u], p_sems, u)
            for k in range(rows_n - 1):
                settle_parts(k)
        parts_in(e)
        own_strip(e)
        strip_product(e)
    for u in range(gpr):
        php_v[u * HALF:(u + 1) * HALF, :] = jnp.dot(
            hpt[...], ptr[:, u * HALF:(u + 1) * HALF], preferred_element_type=F32).T
        rows = slice(u * HALF, (u + 1) * HALF)
        pltpu.make_async_copy(php_v.at[rows], php_out.at[rows], out_s.at[u]).start()
    settle_parts(rows_n - 1)
    dens_load.wait()
    for u in range(gpr):
        rows = slice(u * HALF, (u + 1) * HALF)
        pltpu.make_async_copy(php_v.at[rows], php_out.at[rows], out_s.at[u]).wait()


def hand_over(dens_in, php_in, dens_out, php_out, dens_v, php_v, sems):
    into, out = [], []
    for k, (src, held, dst) in enumerate(((php_in, php_v, php_out), (dens_in, dens_v, dens_out))):
        rows = src.shape[0] // PIECES
        for n in range(PIECES):
            part = slice(n * rows, (n + 1) * rows)
            into.append(pltpu.make_async_copy(src.at[part], held.at[part], sems.at[0, k, n]))
            out.append(pltpu.make_async_copy(held.at[part], dst.at[part], sems.at[1, k, n]))
    for copy in into:
        copy.start()
    for first, second in zip(into, out):
        first.wait()
        second.start()
    for copy in out:
        copy.wait()


def per_device(hamiltonian, pattern, tile_lists, orders, shift):
    rows_n = lax.axis_size("row")
    cols_n = lax.axis_size("col")
    high, wide = hamiltonian.shape
    gpr = high // HALF
    groups = rows_n * gpr
    width = wide // rows_n
    pairs_n = cols_n // 2
    solvers = tile_lists.shape[0]
    blocks = pattern.shape[0]
    dma = pltpu.SemaphoreType.DMA
    smem = pltpu.SMEM
    hbm = pl.BlockSpec(memory_space=pltpu.HBM)
    order = rows_n * high
    scratch = [
        pltpu.VMEM((cols_n, order // TILE, TILE, wide), BF),
        pltpu.VMEM((SPAN, SPAN), BF),
        pltpu.VMEM((SPAN, SPAN), BF),
        pltpu.VMEM((SPAN, SPAN), BF),
        pltpu.VMEM((MAXT, width, TILE), BF),
        pltpu.VMEM((groups, wide, TILE), BF),
        pltpu.VMEM((cols_n, gpr, wide, TILE), BF),
        pltpu.VMEM((groups, wide, HALF), BF),
        pltpu.VMEM((order, high), BF),
        pltpu.VMEM((wide, order), F32),
        pltpu.VMEM((wide, order), BF),
    ]
    results = pl.pallas_call(
        functools.partial(kernel, rows_n, cols_n),
        out_shape=(
            jax.ShapeDtypeStruct((high, wide), BF),
            jax.ShapeDtypeStruct((high, wide), F32),
        ),
        in_specs=[hbm] * 5,
        out_specs=(hbm, hbm),
        scratch_shapes=[
            pltpu.VMEM((high, wide), BF),
            smem((MAXT, solvers), jnp.int32),
            smem((solvers,), jnp.int32),
            smem((blocks, blocks), jnp.int32),
            smem((1,), F32),
            pltpu.VMEM((MAXT, solvers), jnp.int32),
            pltpu.VMEM((groups, solvers), jnp.int32),
            smem((groups, solvers), jnp.int32),
            dma((7,)),
            pltpu.VMEM((high, wide), BF),
            pltpu.VMEM((high, wide), F32),
            dma((gpr + 1,)),
            *scratch,
            *[dma((rows_n * TPC,))] * 3,
            dma((pairs_n,)), dma, dma((rows_n, 2)), *[dma((rows_n,))] * 3,
            *[dma((pairs_n, rows_n * TPC))] * 4,
            *[dma((rows_n, rows_n))] * 2,
            *[dma((pairs_n, gpr))] * 4,
        ],
        compiler_params=pltpu.CompilerParams(
            collective_id=0, has_side_effects=True, vmem_limit_bytes=60000000),
    )(tile_lists.T, orders, pattern, shift, hamiltonian)
    return pl.pallas_call(
        hand_over,
        out_shape=tuple(jax.ShapeDtypeStruct(r.shape, r.dtype) for r in results),
        in_specs=[hbm] * 2,
        out_specs=(hbm, hbm),
        scratch_shapes=[*(pltpu.VMEM(r.shape, r.dtype) for r in results), dma((2, 2, PIECES))],
    )(*results)


def solution(mesh):
    in_specs = (P("row", "col"), P(), P(), P(), P())
    out_specs = (P("row", "col"), P("row", "col"))
    return jax.shard_map(
        per_device, mesh=mesh, in_specs=in_specs, out_specs=out_specs, check_vma=False
    )
```

```python
import functools

import jax
import jax.numpy as jnp
from jax import lax
from jax.experimental import pallas as pl
from jax.experimental.pallas import tpu as pltpu
from jax.sharding import PartitionSpec as P

TILE = 128
TPC = 2
MAXT = 8
BF = jnp.bfloat16
F32 = jnp.float32
MESH = pl.DeviceIdType.MESH
SPAN = MAXT * TILE
HALF = TPC * TILE
PIECES = 2


def eye_block(rows, cols, shift):
    r = lax.broadcasted_iota(jnp.int32, (rows, cols), 0)
    c = lax.broadcasted_iota(jnp.int32, (rows, cols), 1)
    return r == c + shift


def symmetric(left, right, out, finish):
    for n in range(SPAN // HALF):
        cols = slice(n * HALF, (n + 1) * HALF)
        prod = jnp.dot(left[0:(n + 1) * HALF, :], right[:, cols], preferred_element_type=F32)
        done = finish(prod, n)
        out[0:(n + 1) * HALF, cols] = done
        if n:
            out[cols, 0:n * HALF] = done[0:n * HALF, :].T


def kernel(
    rows_n, cols_n, lists_hbm, orders_hbm, pattern_hbm, shift_hbm, ham_hbm,
    dens_out, php_out,
    ham, lists, orders, pattern, shift, lists_v, code_v, code, in_s, dens_v, php_v, out_s, hful, xa, xb, fb, cent, call, pall, ptc, ptr, acc, hpt,
    zu_s, zd_s, z_r, sx_s, sx_r, sz_s, sz_r, sp_s, sp_r, an_s, an_r, ap_s, ap_r, c_s, c_r,
    pn_s, pn_r, pp_s, pp_r,
):
    me_row = lax.axis_index("row")
    me_col = lax.axis_index("col")
    high, wide = ham.shape
    gpr = high // HALF
    groups = rows_n * gpr
    width = wide // rows_n
    pairs_n = cols_n // 2
    bits = pairs_n.bit_length() - 1
    my_pair = me_col // 2
    parity = lax.rem(me_col, 2)
    partner = my_pair * 2 + 1 - parity
    solver = me_col * rows_n + me_row

    def send(src, dst, ss, rs, row, col):
        return pltpu.make_async_remote_copy(
            src_ref=src, dst_ref=dst, send_sem=ss, recv_sem=rs,
            device_id=(row, col), device_id_type=MESH,
        )

    loads = [pltpu.make_async_copy(src, dst, in_s.at[k]) for k, (src, dst) in enumerate((
        (ham_hbm, ham), (pattern_hbm, pattern), (lists_hbm, lists_v), (lists_hbm, lists),
        (orders_hbm, orders), (shift_hbm, shift)))]
    for load in loads:
        load.start()

    barrier = pltpu.get_barrier_semaphore()
    for d in range(1, rows_n):
        pl.semaphore_signal(
            barrier, inc=1, device_id=(lax.rem(me_row + d, rows_n), me_col), device_id_type=MESH)
    for d in range(1, cols_n):
        pl.semaphore_signal(
            barrier, inc=1, device_id=(me_row, lax.rem(me_col + d, cols_n)), device_id_type=MESH)
    pl.semaphore_wait(barrier, rows_n - 1 + cols_n - 1)

    def first(q, c):
        p = c // 2
        par = lax.rem(c, 2)
        return jnp.where(q == p, 0, jnp.where(q < p, par, 1 - par))

    def flip(e, par):
        out = 0
        for j in range(bits):
            b = lax.rem(my_pair // (1 << j), 2)
            c0, c1 = (e >> j) & 1, (e >> (bits - 1 - j)) & 1
            if c0 == c1:
                b = 1 - b if c0 else b
            else:
                t = 1 - par if c0 else par
                b = b + t - 2 * b * t
            out = out + (1 << j) * b
        return out

    def column(e, par):
        return flip(e, par) * 2 + par

    def later(e):
        return [i for i in range(bits) if (1 << i) > e]

    def strip_rows(g):
        return pl.ds(g * TPC, TPC)

    below = jnp.where(me_row < rows_n - 1 - me_row, me_row, rows_n - 1 - me_row)
    rest = jnp.where(me_row < rows_n - 1 - me_row, 1, -1)

    def row_at(t):
        near = me_row + (t + 1) // 2 if t % 2 else me_row - t // 2
        return jnp.where(t <= 2 * below, near, me_row + rest * (t - below))

    def group_of(q, c):
        return q * gpr + first(q, c)

    def turn(q, c):
        g = group_of(q, c)

        @pl.when(g != c)
        def _():
            hful[g, strip_rows(c)] = hful[c, strip_rows(g)].reshape(HALF, HALF).T.reshape(
                TPC, TILE, HALF)

    def net(src, dst, ss, rs, e, t, i):
        f = e | (1 << i)
        return send(src, dst, ss.at[f, t], rs.at[f, t], me_row, column(1 << i, parity))

    def pass_on(src, dst, ss, rs, e, t):
        return send(src, dst, ss.at[e, t], rs.at[e, t], me_row, partner)

    def forward(src, dst, sems, e, t):
        ns, nr, ps, pr = sems
        for i in later(e):
            net(src, dst, ns, nr, e, t, i).start()
        pass_on(src, dst, ps, pr, e, t).start()

    def from_net(ref, sems, e, t):
        ns, nr, ps, pr = sems
        top = e.bit_length() - 1
        net(ref, ref, ns, nr, e ^ (1 << top), t, top).wait_recv()
        forward(ref, ref, sems, e, t)

    def from_partner(ref, sems, e, t):
        ns, nr, ps, pr = sems
        pass_on(ref, ref, ps, pr, e, t).wait_recv()

    def drain(ref, sems, t):
        ns, nr, ps, pr = sems
        for e in range(pairs_n):
            for i in later(e):
                net(ref, ref, ns, nr, e, t, i).wait_send()
            pass_on(ref, ref, ps, pr, e, t).wait_send()

    a_sems = (an_s, an_r, ap_s, ap_r)

    def keep_own(half, g):
        for a in range(TPC):
            for b in range(TPC):
                ga = g * TPC + a
                gb = me_col * TPC + b
                keep = (pattern[ga, gb] == 1) | (ga == gb)
                t = ham[pl.ds(pl.multiple_of(half * HALF + a * TILE, TILE), TILE),
                        b * TILE:(b + 1) * TILE]
                hful[me_col, g * TPC + a, :, b * TILE:(b + 1) * TILE] = jnp.where(
                    keep, t, jnp.zeros_like(t))

    loads[0].wait()
    loads[1].wait()
    my_half = first(me_row, me_col)
    keep_own(my_half, me_row * gpr + my_half)

    def along(ref, ss, rs, sign):
        return send(ref, ref, ss, rs, me_row + sign, me_col)

    def relay(q, make):
        @pl.when((q <= me_row) & (me_row < rows_n - 1))
        def _():
            make(1)

        @pl.when((q >= me_row) & (me_row > 0))
        def _():
            make(-1)

    stream = [(t, h) for t in range(rows_n) for h in range(TPC)]

    def piece(t, h, c):
        return hful.at[c, group_of(row_at(t), c) * TPC + h]

    def index(t, h):
        return row_at(t) * TPC + h

    def z_copy(t, h, sign):
        k = index(t, h)
        return along(piece(t, h, me_col), (zu_s if sign > 0 else zd_s).at[k], z_r.at[k], sign)

    def z_send(t, h):
        relay(row_at(t), lambda sign: z_copy(t, h, sign).start())

    def second(p):
        c = p * 2 + 1
        return hful.at[c, strip_rows(c)]

    def sx_copy(i):
        return send(second(me_row), second(me_row), sx_s.at[i], sx_r, me_row, column(1 << i, parity))

    def sz_copy(p, sign):
        return along(second(p), sz_s.at[p, (sign + 1) // 2], sz_r.at[p], sign)

    def sp_copy(p):
        return send(second(p), second(p), sp_s.at[p], sp_r.at[p], me_row, partner)

    def at_hop(some, do):
        for e in some:
            @pl.when((parity == 1) & (flip(e, parity) == me_row))
            def _():
                do(e)

    def onward(p):
        relay(p, lambda sign: sz_copy(p, sign).start())
        sp_copy(p).start()

    def second_in_row(e):
        if e:
            sx_copy(0).wait_recv()
        for i in later(e):
            sx_copy(i).start()
        onward(me_row)

    def second_along(t):
        @pl.when(parity == 1)
        def _():
            sz_copy(row_at(t), 1).wait_recv()
            onward(row_at(t))

    for h in range(TPC):
        z_send(0, h)
        ref = piece(0, h, me_col)
        forward(ref, ref, a_sems, 0, index(0, h))

    def start_second(e):
        keep_own(1, me_col)
        second_in_row(e)
    at_hop([0], start_second)
    turn(me_row, me_col)

    for load in loads[2:]:
        load.wait()
    tiles = lists_v[...]
    place_of = lax.broadcasted_iota(jnp.int32, tiles.shape, 0) * TPC + lax.rem(tiles, TPC)
    for g in range(groups):
        code_v[g:g + 1, :] = jnp.max(
            jnp.where(tiles // TPC == g, place_of, -1), axis=0, keepdims=True)
    code_load = pltpu.make_async_copy(code_v, code, in_s.at[len(loads)])
    code_load.start()

    def enter(t, h):
        if t:
            z_copy(t, h, 1).wait_recv()
            z_send(t, h)
            ref = piece(t, h, me_col)
            forward(ref, ref, a_sems, 0, index(t, h))
            if h == TPC - 1:
                turn(row_at(t), me_col)

    def arrive(t, h, some):
        for e in some:
            c = column(e, parity)
            from_net(piece(t, h, c), a_sems, e, index(t, h))
            if h == TPC - 1:
                turn(row_at(t), c)

    def handed(t, h):
        for e in range(pairs_n):
            c = column(e, 1 - parity)
            from_partner(piece(t, h, c), a_sems, e, index(t, h))
            if h == TPC - 1:
                turn(row_at(t), c)

    by_hops = [[e for e in range(1, pairs_n) if bin(e).count("1") == k] for k in range(1, bits + 1)]
    lags = [(2 * k, by_hops[k - 1]) for k in range(1, bits + 1)]
    for i in range(len(stream) + 4 * bits):
        if i < len(stream):
            enter(*stream[i])
        for lag, some in lags:
            if 0 <= i - lag < len(stream):
                arrive(*stream[i - lag], some)
        k = i - 1
        if 1 <= k <= bits:
            at_hop(by_hops[k - 1], second_in_row)
        if 1 <= k - bits < rows_n:
            second_along(k - bits)
        if 0 <= i - 4 * bits < len(stream):
            handed(*stream[i - 4 * bits])

    @pl.when(parity == 0)
    def _():
        for p in range(rows_n):
            sp_copy(p).wait_recv()

    code_load.wait()

    potential = shift[0]
    order = orders[solver]
    biggest = jnp.zeros((TILE, 1), F32)
    on_diag = eye_block(TILE, TILE, 0)
    for i in range(MAXT):
        ti = lists[i, solver]
        total = jnp.zeros((TILE, TILE), F32)
        for j in range(MAXT):
            tj = lists[j, solver]
            both = hful[tj // TPC, ti]
            w = jnp.where(lax.rem(tj, TPC) == 1, both[:, TILE:], both[:, :TILE])
            w = jnp.where((i < order) & (j < order), w, jnp.zeros_like(w))
            v = w.astype(F32)
            if i == j:
                move = jnp.where(i < order, potential, 0.0)
                v = v - jnp.where(on_diag, move, 0.0)
                w = v.astype(BF)
            xa[i * TILE:(i + 1) * TILE, j * TILE:(j + 1) * TILE] = w
            total = total + v * v
        biggest = jnp.maximum(biggest, jnp.sum(total, axis=1, keepdims=True))
    top = jnp.max(biggest, axis=0, keepdims=True)
    scale = jnp.abs(potential) + 2.0 * jnp.sqrt(top + 1e-06)
    inverse = 1.0 / scale
    lead = 1.5 * inverse
    tail = 0.5 * inverse * inverse * inverse

    def plain(prod, n):
        return prod.astype(BF)

    def upper(ref, n):
        return ref[0:(n + 1) * HALF, n * HALF:(n + 1) * HALF].astype(F32)

    symmetric(xa, xa, fb, plain)
    symmetric(xa, fb, xb, lambda prod, n: (lead * upper(xa, n) - tail * prod).astype(BF))
    symmetric(xb, xb, fb, plain)
    symmetric(xb, fb, xa, lambda prod, n: (1.5 * upper(xb, n) - 0.5 * prod).astype(BF))

    offset = pl.multiple_of(lax.rem(solver * width, TILE), width)
    hit = lax.broadcasted_iota(jnp.int32, (width, SPAN), 0) + offset == lax.broadcasted_iota(
        jnp.int32, (width, SPAN), 1)
    part = xa[pl.ds(offset, width), :]
    q = jnp.dot(part, xa[...], preferred_element_type=F32)
    f = (jnp.where(hit, 1.5, 0.0) - 0.5 * q).astype(BF)
    y = jnp.dot(f, xa[...], preferred_element_type=F32)
    dens = (0.5 * (jnp.where(hit, 1.0, 0.0) - y)).astype(BF)
    for i in range(MAXT):
        cent[i] = dens[:, i * TILE:(i + 1) * TILE]

    my_rows = pl.ds(pl.multiple_of(me_row * width, width), width)

    def code_of(g, s):
        cd = code[g, s]
        return jnp.where(jnp.maximum(cd, 0) // TPC < orders[s], cd, -1)

    def place(g, carry):
        where = code_of(g, solver)
        t = cent[jnp.maximum(where, 0) // 2]
        call[g, my_rows, :] = jnp.where(where >= 0, t, jnp.zeros_like(t))
        return carry
    lax.fori_loop(0, groups, place, 0)

    def part(e, d):
        to = lax.rem(me_row + d, rows_n)
        p = lax.rem(me_row + d + e, rows_n)
        ref = call.at[pl.ds(p * gpr, gpr), my_rows, :]
        return send(ref, ref, c_s.at[e, d], c_r.at[e, d], to, me_col)

    def part_in(e, d):
        q = lax.rem(me_row + rows_n - d, rows_n)
        p = lax.rem(me_row + e, rows_n)
        ref = call.at[pl.ds(p * gpr, gpr), pl.ds(pl.multiple_of(q * width, width), width), :]
        return send(ref, ref, c_s.at[e, d], c_r.at[e, d], lax.rem(me_row + d, rows_n), me_col)

    def parts_out(e):
        if e < rows_n:
            for d in range(1, rows_n):
                part(e, d).start()

    def parts_in(e):
        for d in range(1, rows_n):
            part_in(e, d).wait_recv()
        parts_out(e + 2)

    parts_out(0)
    parts_out(1)

    p_sems = (pn_s, pn_r, pp_s, pp_r)

    parts_in(0)
    for u in range(gpr):
        forward(call.at[me_row * gpr + u], pall.at[me_col, u], p_sems, 0, u)

    def halves(v, s, g, rows, store):
        cd = code_of(g, s)
        for h in range(TPC):
            ok = (cd >= 0) & (lax.rem(jnp.maximum(cd, 0), 2) == h)
            store(rows, h, jnp.where(ok, v, jnp.zeros_like(v)))

    def spread(src, c, u):
        for q in range(rows_n):
            def store(rows, h, v):
                ptr[pl.ds(pl.multiple_of(c * wide + q * width, width), width),
                    u * HALF + h * TILE:u * HALF + (h + 1) * TILE] = v
            halves(src[q * width:(q + 1) * width, :], c * rows_n + q, me_row * gpr + u, None, store)

    def own_strip(e):
        for u in range(gpr):
            g = lax.rem(me_row + e, rows_n) * gpr + u
            for q in range(rows_n):
                def store(rows, h, v):
                    ptc[g, q * width:(q + 1) * width, h * TILE:(h + 1) * TILE] = v
                halves(call[g, q * width:(q + 1) * width, :], me_col * rows_n + q, g, None, store)

    own_strip(0)
    for u in range(gpr):
        spread(call.at[me_row * gpr + u], me_col, u)
        dens_v[u * HALF:(u + 1) * HALF, :] = ptc[me_row * gpr + u].T

    dens_load = pltpu.make_async_copy(dens_v, dens_out, out_s.at[gpr])
    dens_load.start()

    def strips(some):
        for e in some:
            c = column(e, parity)
            for u in range(gpr):
                from_net(pall.at[c, u], p_sems, e, u)
                spread(pall.at[c, u], c, u)

    def strips_handed():
        for e in range(pairs_n):
            c = column(e, 1 - parity)
            for u in range(gpr):
                from_partner(pall.at[c, u], p_sems, e, u)
                spread(pall.at[c, u], c, u)

    def strip_product(e):
        p = lax.rem(me_row + e, rows_n)

        def some(h, carry):
            cols = pl.ds(pl.multiple_of(h * HALF, HALF), HALF)
            total = jnp.zeros((wide, HALF), F32) if e == 0 else acc[:, cols]
            for u in range(gpr):
                g = p * gpr + u
                total = total + jnp.dot(
                    ptc[g], hful[h, strip_rows(g)].reshape(HALF, HALF), preferred_element_type=F32)
            if e == rows_n - 1:
                hpt[:, cols] = total.astype(BF)
            else:
                acc[:, cols] = total
            return carry
        lax.fori_loop(0, groups, some, 0, unroll=4)

    def settle_blocks():
        for t, h in stream:
            drain(piece(0, h, me_col), a_sems, index(t, h))
            relay(row_at(t), lambda sign: z_copy(t, h, sign).wait_send())

        for e in range(pairs_n):
            def sent(e):
                for i in later(e):
                    sx_copy(i).wait_send()
            at_hop([e], sent)

        @pl.when(parity == 1)
        def _():
            for t in range(rows_n):
                relay(row_at(t), lambda sign: sz_copy(row_at(t), sign).wait_send())
                sp_copy(row_at(t)).wait_send()

    def settle_parts(e):
        for d in range(1, rows_n):
            part(e, d).wait_send()

    strip_product(0)
    settle_blocks()
    for e in range(1, rows_n):
        if e <= bits:
            strips(by_hops[e - 1])
        if e == rows_n - 1:
            for k in range(e, bits):
                strips(by_hops[k])
            strips_handed()
            for u in range(gpr):
                drain(pall.at[me_col, u], p_sems, u)
            for k in range(rows_n - 1):
                settle_parts(k)
        parts_in(e)
        own_strip(e)
        strip_product(e)
    for u in range(gpr):
        php_v[u * HALF:(u + 1) * HALF, :] = jnp.dot(
            hpt[...], ptr[:, u * HALF:(u + 1) * HALF], preferred_element_type=F32).T
        rows = slice(u * HALF, (u + 1) * HALF)
        pltpu.make_async_copy(php_v.at[rows], php_out.at[rows], out_s.at[u]).start()
    settle_parts(rows_n - 1)
    dens_load.wait()
    for u in range(gpr):
        rows = slice(u * HALF, (u + 1) * HALF)
        pltpu.make_async_copy(php_v.at[rows], php_out.at[rows], out_s.at[u]).wait()


def hand_over(dens_in, php_in, dens_out, php_out, dens_v, php_v, sems):
    into, out = [], []
    for k, (src, held, dst) in enumerate(((php_in, php_v, php_out), (dens_in, dens_v, dens_out))):
        rows = src.shape[0] // PIECES
        for n in range(PIECES):
            part = slice(n * rows, (n + 1) * rows)
            into.append(pltpu.make_async_copy(src.at[part], held.at[part], sems.at[0, k, n]))
            out.append(pltpu.make_async_copy(held.at[part], dst.at[part], sems.at[1, k, n]))
    for copy in into:
        copy.start()
    for first, second in zip(into, out):
        first.wait()
        second.start()
    for copy in out:
        copy.wait()


def per_device(hamiltonian, pattern, tile_lists, orders, shift):
    rows_n = lax.axis_size("row")
    cols_n = lax.axis_size("col")
    high, wide = hamiltonian.shape
    gpr = high // HALF
    groups = rows_n * gpr
    width = wide // rows_n
    pairs_n = cols_n // 2
    solvers = tile_lists.shape[0]
    blocks = pattern.shape[0]
    dma = pltpu.SemaphoreType.DMA
    smem = pltpu.SMEM
    hbm = pl.BlockSpec(memory_space=pltpu.HBM)
    order = rows_n * high
    scratch = [
        pltpu.VMEM((cols_n, order // TILE, TILE, wide), BF),
        pltpu.VMEM((SPAN, SPAN), BF),
        pltpu.VMEM((SPAN, SPAN), BF),
        pltpu.VMEM((SPAN, SPAN), BF),
        pltpu.VMEM((MAXT, width, TILE), BF),
        pltpu.VMEM((groups, wide, TILE), BF),
        pltpu.VMEM((cols_n, gpr, wide, TILE), BF),
        pltpu.VMEM((groups, wide, HALF), BF),
        pltpu.VMEM((order, high), BF),
        pltpu.VMEM((wide, order), F32),
        pltpu.VMEM((wide, order), BF),
    ]
    results = pl.pallas_call(
        functools.partial(kernel, rows_n, cols_n),
        out_shape=(
            jax.ShapeDtypeStruct((high, wide), BF),
            jax.ShapeDtypeStruct((high, wide), F32),
        ),
        in_specs=[hbm] * 5,
        out_specs=(hbm, hbm),
        scratch_shapes=[
            pltpu.VMEM((high, wide), BF),
            smem((MAXT, solvers), jnp.int32),
            smem((solvers,), jnp.int32),
            smem((blocks, blocks), jnp.int32),
            smem((1,), F32),
            pltpu.VMEM((MAXT, solvers), jnp.int32),
            pltpu.VMEM((groups, solvers), jnp.int32),
            smem((groups, solvers), jnp.int32),
            dma((7,)),
            pltpu.VMEM((high, wide), BF),
            pltpu.VMEM((high, wide), F32),
            dma((gpr + 1,)),
            *scratch,
            *[dma((rows_n * TPC,))] * 3,
            dma((pairs_n,)), dma, dma((rows_n, 2)), *[dma((rows_n,))] * 3,
            *[dma((pairs_n, rows_n * TPC))] * 4,
            *[dma((rows_n, rows_n))] * 2,
            *[dma((pairs_n, gpr))] * 4,
        ],
        compiler_params=pltpu.CompilerParams(
            collective_id=0, has_side_effects=True, vmem_limit_bytes=60000000),
    )(tile_lists.T, orders, pattern, shift, hamiltonian)
    return pl.pallas_call(
        hand_over,
        out_shape=tuple(jax.ShapeDtypeStruct(r.shape, r.dtype) for r in results),
        in_specs=[hbm] * 2,
        out_specs=(hbm, hbm),
        scratch_shapes=[*(pltpu.VMEM(r.shape, r.dtype) for r in results), dma((2, 2, PIECES))],
    )(*results)


def solution(mesh):
    in_specs = (P("row", "col"), P(), P(), P(), P())
    out_specs = (P("row", "col"), P("row", "col"))
    return jax.shard_map(
        per_device, mesh=mesh, in_specs=in_specs, out_specs=out_specs, check_vma=False
    )
```

```python
import functools

import jax
import jax.numpy as jnp
from jax import lax
from jax.experimental import pallas as pl
from jax.experimental.pallas import tpu as pltpu
from jax.sharding import PartitionSpec as P

TILE = 128
TPC = 2
MAXT = 8
BF = jnp.bfloat16
F32 = jnp.float32
MESH = pl.DeviceIdType.MESH
SPAN = MAXT * TILE
HALF = TPC * TILE
PIECES = 2


def eye_block(rows, cols, shift):
    r = lax.broadcasted_iota(jnp.int32, (rows, cols), 0)
    c = lax.broadcasted_iota(jnp.int32, (rows, cols), 1)
    return r == c + shift


def symmetric(left, right, out, finish):
    for n in range(SPAN // HALF):
        cols = slice(n * HALF, (n + 1) * HALF)
        prod = jnp.dot(left[0:(n + 1) * HALF, :], right[:, cols], preferred_element_type=F32)
        done = finish(prod, n)
        out[0:(n + 1) * HALF, cols] = done
        if n:
            out[cols, 0:n * HALF] = done[0:n * HALF, :].T


def kernel(
    rows_n, cols_n, lists_hbm, orders_hbm, pattern_hbm, shift_hbm, ham_hbm,
    dens_out, php_out,
    ham, lists, orders, pattern, shift, lists_v, code_v, code, in_s, dens_v, php_v, out_s, hful, xa, xb, fb, cent, call, pall, ptc, ptr, acc, hpt,
    zu_s, zd_s, z_r, sx_s, sx_r, sz_s, sz_r, sp_s, sp_r, an_s, an_r, ap_s, ap_r, c_s, c_r,
    pn_s, pn_r, pp_s, pp_r,
):
    me_row = lax.axis_index("row")
    me_col = lax.axis_index("col")
    high, wide = ham.shape
    gpr = high // HALF
    groups = rows_n * gpr
    width = wide // rows_n
    pairs_n = cols_n // 2
    bits = pairs_n.bit_length() - 1
    my_pair = me_col // 2
    parity = lax.rem(me_col, 2)
    partner = my_pair * 2 + 1 - parity
    solver = me_col * rows_n + me_row

    def send(src, dst, ss, rs, row, col):
        return pltpu.make_async_remote_copy(
            src_ref=src, dst_ref=dst, send_sem=ss, recv_sem=rs,
            device_id=(row, col), device_id_type=MESH,
        )

    loads = [pltpu.make_async_copy(src, dst, in_s.at[k]) for k, (src, dst) in enumerate((
        (ham_hbm, ham), (pattern_hbm, pattern), (lists_hbm, lists_v), (lists_hbm, lists),
        (orders_hbm, orders), (shift_hbm, shift)))]
    for load in loads:
        load.start()

    barrier = pltpu.get_barrier_semaphore()
    for d in range(1, rows_n):
        pl.semaphore_signal(
            barrier, inc=1, device_id=(lax.rem(me_row + d, rows_n), me_col), device_id_type=MESH)
    for d in range(1, cols_n):
        pl.semaphore_signal(
            barrier, inc=1, device_id=(me_row, lax.rem(me_col + d, cols_n)), device_id_type=MESH)
    pl.semaphore_wait(barrier, rows_n - 1 + cols_n - 1)

    def first(q, c):
        p = c // 2
        par = lax.rem(c, 2)
        return jnp.where(q == p, 0, jnp.where(q < p, par, 1 - par))

    def flip(e, par):
        out = 0
        for j in range(bits):
            b = lax.rem(my_pair // (1 << j), 2)
            c0, c1 = (e >> j) & 1, (e >> (bits - 1 - j)) & 1
            if c0 == c1:
                b = 1 - b if c0 else b
            else:
                t = 1 - par if c0 else par
                b = b + t - 2 * b * t
            out = out + (1 << j) * b
        return out

    def column(e, par):
        return flip(e, par) * 2 + par

    def later(e):
        return [i for i in range(bits) if (1 << i) > e]

    def strip_rows(g):
        return pl.ds(g * TPC, TPC)

    below = jnp.where(me_row < rows_n - 1 - me_row, me_row, rows_n - 1 - me_row)
    rest = jnp.where(me_row < rows_n - 1 - me_row, 1, -1)

    def row_at(t):
        near = me_row + (t + 1) // 2 if t % 2 else me_row - t // 2
        return jnp.where(t <= 2 * below, near, me_row + rest * (t - below))

    def group_of(q, c):
        return q * gpr + first(q, c)

    def turn(q, c):
        g = group_of(q, c)

        @pl.when(g != c)
        def _():
            hful[g, strip_rows(c)] = hful[c, strip_rows(g)].reshape(HALF, HALF).T.reshape(
                TPC, TILE, HALF)

    def net(src, dst, ss, rs, e, t, i):
        f = e | (1 << i)
        return send(src, dst, ss.at[f, t], rs.at[f, t], me_row, column(1 << i, parity))

    def pass_on(src, dst, ss, rs, e, t):
        return send(src, dst, ss.at[e, t], rs.at[e, t], me_row, partner)

    def forward(src, dst, sems, e, t):
        ns, nr, ps, pr = sems
        for i in later(e):
            net(src, dst, ns, nr, e, t, i).start()
        pass_on(src, dst, ps, pr, e, t).start()

    def from_net(ref, sems, e, t):
        ns, nr, ps, pr = sems
        top = e.bit_length() - 1
        net(ref, ref, ns, nr, e ^ (1 << top), t, top).wait_recv()
        forward(ref, ref, sems, e, t)

    def from_partner(ref, sems, e, t):
        ns, nr, ps, pr = sems
        pass_on(ref, ref, ps, pr, e, t).wait_recv()

    def drain(ref, sems, t):
        ns, nr, ps, pr = sems
        for e in range(pairs_n):
            for i in later(e):
                net(ref, ref, ns, nr, e, t, i).wait_send()
            pass_on(ref, ref, ps, pr, e, t).wait_send()

    a_sems = (an_s, an_r, ap_s, ap_r)

    def keep_own(half, g):
        for a in range(TPC):
            for b in range(TPC):
                ga = g * TPC + a
                gb = me_col * TPC + b
                keep = (pattern[ga, gb] == 1) | (ga == gb)
                t = ham[pl.ds(pl.multiple_of(half * HALF + a * TILE, TILE), TILE),
                        b * TILE:(b + 1) * TILE]
                hful[me_col, g * TPC + a, :, b * TILE:(b + 1) * TILE] = jnp.where(
                    keep, t, jnp.zeros_like(t))

    loads[0].wait()
    loads[1].wait()
    my_half = first(me_row, me_col)
    keep_own(my_half, me_row * gpr + my_half)

    def along(ref, ss, rs, sign):
        return send(ref, ref, ss, rs, me_row + sign, me_col)

    def relay(q, make):
        @pl.when((q <= me_row) & (me_row < rows_n - 1))
        def _():
            make(1)

        @pl.when((q >= me_row) & (me_row > 0))
        def _():
            make(-1)

    stream = [(t, h) for t in range(rows_n) for h in range(TPC)]

    def piece(t, h, c):
        return hful.at[c, group_of(row_at(t), c) * TPC + h]

    def index(t, h):
        return row_at(t) * TPC + h

    def z_copy(t, h, sign):
        k = index(t, h)
        return along(piece(t, h, me_col), (zu_s if sign > 0 else zd_s).at[k], z_r.at[k], sign)

    def z_send(t, h):
        relay(row_at(t), lambda sign: z_copy(t, h, sign).start())

    def second(p):
        c = p * 2 + 1
        return hful.at[c, strip_rows(c)]

    def sx_copy(i):
        return send(second(me_row), second(me_row), sx_s.at[i], sx_r, me_row, column(1 << i, parity))

    def sz_copy(p, sign):
        return along(second(p), sz_s.at[p, (sign + 1) // 2], sz_r.at[p], sign)

    def sp_copy(p):
        return send(second(p), second(p), sp_s.at[p], sp_r.at[p], me_row, partner)

    def at_hop(some, do):
        for e in some:
            @pl.when((parity == 1) & (flip(e, parity) == me_row))
            def _():
                do(e)

    def onward(p):
        relay(p, lambda sign: sz_copy(p, sign).start())
        sp_copy(p).start()

    def second_in_row(e):
        if e:
            sx_copy(0).wait_recv()
        for i in later(e):
            sx_copy(i).start()
        onward(me_row)

    def second_along(t):
        @pl.when(parity == 1)
        def _():
            sz_copy(row_at(t), 1).wait_recv()
            onward(row_at(t))

    for h in range(TPC):
        z_send(0, h)
        ref = piece(0, h, me_col)
        forward(ref, ref, a_sems, 0, index(0, h))

    def start_second(e):
        keep_own(1, me_col)
        second_in_row(e)
    at_hop([0], start_second)
    turn(me_row, me_col)

    for load in loads[2:]:
        load.wait()
    tiles = lists_v[...]
    place_of = lax.broadcasted_iota(jnp.int32, tiles.shape, 0) * TPC + lax.rem(tiles, TPC)
    for g in range(groups):
        code_v[g:g + 1, :] = jnp.max(
            jnp.where(tiles // TPC == g, place_of, -1), axis=0, keepdims=True)
    code_load = pltpu.make_async_copy(code_v, code, in_s.at[len(loads)])
    code_load.start()

    def enter(t, h):
        if t:
            z_copy(t, h, 1).wait_recv()
            z_send(t, h)
            ref = piece(t, h, me_col)
            forward(ref, ref, a_sems, 0, index(t, h))
            if h == TPC - 1:
                turn(row_at(t), me_col)

    def arrive(t, h, some):
        for e in some:
            c = column(e, parity)
            from_net(piece(t, h, c), a_sems, e, index(t, h))
            if h == TPC - 1:
                turn(row_at(t), c)

    def handed(t, h):
        for e in range(pairs_n):
            c = column(e, 1 - parity)
            from_partner(piece(t, h, c), a_sems, e, index(t, h))
            if h == TPC - 1:
                turn(row_at(t), c)

    by_hops = [[e for e in range(1, pairs_n) if bin(e).count("1") == k] for k in range(1, bits + 1)]
    lags = [(2 * k, by_hops[k - 1]) for k in range(1, bits + 1)]
    for i in range(len(stream) + 4 * bits):
        if i < len(stream):
            enter(*stream[i])
        for lag, some in lags:
            if 0 <= i - lag < len(stream):
                arrive(*stream[i - lag], some)
        k = i - 1
        if 1 <= k <= bits:
            at_hop(by_hops[k - 1], second_in_row)
        if 1 <= k - bits < rows_n:
            second_along(k - bits)
        if 0 <= i - 4 * bits < len(stream):
            handed(*stream[i - 4 * bits])

    @pl.when(parity == 0)
    def _():
        for p in range(rows_n):
            sp_copy(p).wait_recv()

    code_load.wait()

    potential = shift[0]
    order = orders[solver]
    biggest = jnp.zeros((TILE, 1), F32)
    on_diag = eye_block(TILE, TILE, 0)
    for i in range(MAXT):
        ti = lists[i, solver]
        total = jnp.zeros((TILE, TILE), F32)
        for j in range(MAXT):
            tj = lists[j, solver]
            both = hful[tj // TPC, ti]
            w = jnp.where(lax.rem(tj, TPC) == 1, both[:, TILE:], both[:, :TILE])
            w = jnp.where((i < order) & (j < order), w, jnp.zeros_like(w))
            v = w.astype(F32)
            if i == j:
                move = jnp.where(i < order, potential, 0.0)
                v = v - jnp.where(on_diag, move, 0.0)
                w = v.astype(BF)
            xa[i * TILE:(i + 1) * TILE, j * TILE:(j + 1) * TILE] = w
            total = total + v * v
        biggest = jnp.maximum(biggest, jnp.sum(total, axis=1, keepdims=True))
    top = jnp.max(biggest, axis=0, keepdims=True)
    scale = jnp.abs(potential) + 2.0 * jnp.sqrt(top + 1e-06)
    inverse = 1.0 / scale
    lead = 1.5 * inverse
    tail = 0.5 * inverse * inverse * inverse

    def plain(prod, n):
        return prod.astype(BF)

    def upper(ref, n):
        return ref[0:(n + 1) * HALF, n * HALF:(n + 1) * HALF].astype(F32)

    symmetric(xa, xa, fb, plain)
    symmetric(xa, fb, xb, lambda prod, n: (lead * upper(xa, n) - tail * prod).astype(BF))
    symmetric(xb, xb, fb, plain)
    symmetric(xb, fb, xa, lambda prod, n: (1.5 * upper(xb, n) - 0.5 * prod).astype(BF))

    offset = pl.multiple_of(lax.rem(solver * width, TILE), width)
    hit = lax.broadcasted_iota(jnp.int32, (width, SPAN), 0) + offset == lax.broadcasted_iota(
        jnp.int32, (width, SPAN), 1)
    part = xa[pl.ds(offset, width), :]
    q = jnp.dot(part, xa[...], preferred_element_type=F32)
    f = (jnp.where(hit, 1.5, 0.0) - 0.5 * q).astype(BF)
    y = jnp.dot(f, xa[...], preferred_element_type=F32)
    dens = (0.5 * (jnp.where(hit, 1.0, 0.0) - y)).astype(BF)
    for i in range(MAXT):
        cent[i] = dens[:, i * TILE:(i + 1) * TILE]

    my_rows = pl.ds(pl.multiple_of(me_row * width, width), width)

    def code_of(g, s):
        cd = code[g, s]
        return jnp.where(jnp.maximum(cd, 0) // TPC < orders[s], cd, -1)

    def place(g, carry):
        where = code_of(g, solver)
        t = cent[jnp.maximum(where, 0) // 2]
        call[g, my_rows, :] = jnp.where(where >= 0, t, jnp.zeros_like(t))
        return carry
    lax.fori_loop(0, groups, place, 0)

    def part(e, d):
        to = lax.rem(me_row + d, rows_n)
        p = lax.rem(me_row + d + e, rows_n)
        ref = call.at[pl.ds(p * gpr, gpr), my_rows, :]
        return send(ref, ref, c_s.at[e, d], c_r.at[e, d], to, me_col)

    def part_in(e, d):
        q = lax.rem(me_row + rows_n - d, rows_n)
        p = lax.rem(me_row + e, rows_n)
        ref = call.at[pl.ds(p * gpr, gpr), pl.ds(pl.multiple_of(q * width, width), width), :]
        return send(ref, ref, c_s.at[e, d], c_r.at[e, d], lax.rem(me_row + d, rows_n), me_col)

    def parts_out(e):
        if e < rows_n:
            for d in range(1, rows_n):
                part(e, d).start()

    def parts_in(e):
        for d in range(1, rows_n):
            part_in(e, d).wait_recv()
        parts_out(e + 2)

    parts_out(0)
    parts_out(1)

    p_sems = (pn_s, pn_r, pp_s, pp_r)

    parts_in(0)
    for u in range(gpr):
        forward(call.at[me_row * gpr + u], pall.at[me_col, u], p_sems, 0, u)

    def halves(v, s, g, rows, store):
        cd = code_of(g, s)
        for h in range(TPC):
            ok = (cd >= 0) & (lax.rem(jnp.maximum(cd, 0), 2) == h)
            store(rows, h, jnp.where(ok, v, jnp.zeros_like(v)))

    def spread(src, c, u):
        for q in range(rows_n):
            def store(rows, h, v):
                ptr[pl.ds(pl.multiple_of(c * wide + q * width, width), width),
                    u * HALF + h * TILE:u * HALF + (h + 1) * TILE] = v
            halves(src[q * width:(q + 1) * width, :], c * rows_n + q, me_row * gpr + u, None, store)

    def own_strip(e):
        for u in range(gpr):
            g = lax.rem(me_row + e, rows_n) * gpr + u
            for q in range(rows_n):
                def store(rows, h, v):
                    ptc[g, q * width:(q + 1) * width, h * TILE:(h + 1) * TILE] = v
                halves(call[g, q * width:(q + 1) * width, :], me_col * rows_n + q, g, None, store)

    own_strip(0)
    for u in range(gpr):
        spread(call.at[me_row * gpr + u], me_col, u)
        dens_v[u * HALF:(u + 1) * HALF, :] = ptc[me_row * gpr + u].T

    dens_load = pltpu.make_async_copy(dens_v, dens_out, out_s.at[gpr])
    dens_load.start()

    def strips(some):
        for e in some:
            c = column(e, parity)
            for u in range(gpr):
                from_net(pall.at[c, u], p_sems, e, u)
                spread(pall.at[c, u], c, u)

    def strips_handed():
        for e in range(pairs_n):
            c = column(e, 1 - parity)
            for u in range(gpr):
                from_partner(pall.at[c, u], p_sems, e, u)
                spread(pall.at[c, u], c, u)

    def strip_product(e):
        p = lax.rem(me_row + e, rows_n)

        def some(h, carry):
            cols = pl.ds(pl.multiple_of(h * HALF, HALF), HALF)
            total = jnp.zeros((wide, HALF), F32) if e == 0 else acc[:, cols]
            for u in range(gpr):
                g = p * gpr + u
                total = total + jnp.dot(
                    ptc[g], hful[h, strip_rows(g)].reshape(HALF, HALF), preferred_element_type=F32)
            if e == rows_n - 1:
                hpt[:, cols] = total.astype(BF)
            else:
                acc[:, cols] = total
            return carry
        lax.fori_loop(0, groups, some, 0, unroll=8)

    def settle_blocks():
        for t, h in stream:
            drain(piece(0, h, me_col), a_sems, index(t, h))
            relay(row_at(t), lambda sign: z_copy(t, h, sign).wait_send())

        for e in range(pairs_n):
            def sent(e):
                for i in later(e):
                    sx_copy(i).wait_send()
            at_hop([e], sent)

        @pl.when(parity == 1)
        def _():
            for t in range(rows_n):
                relay(row_at(t), lambda sign: sz_copy(row_at(t), sign).wait_send())
                sp_copy(row_at(t)).wait_send()

    def settle_parts(e):
        for d in range(1, rows_n):
            part(e, d).wait_send()

    strip_product(0)
    settle_blocks()
    for e in range(1, rows_n):
        if e <= bits:
            strips(by_hops[e - 1])
        if e == rows_n - 1:
            for k in range(e, bits):
                strips(by_hops[k])
            strips_handed()
            for u in range(gpr):
                drain(pall.at[me_col, u], p_sems, u)
            for k in range(rows_n - 1):
                settle_parts(k)
        parts_in(e)
        own_strip(e)
        strip_product(e)
    for u in range(gpr):
        php_v[u * HALF:(u + 1) * HALF, :] = jnp.dot(
            hpt[...], ptr[:, u * HALF:(u + 1) * HALF], preferred_element_type=F32).T
        rows = slice(u * HALF, (u + 1) * HALF)
        pltpu.make_async_copy(php_v.at[rows], php_out.at[rows], out_s.at[u]).start()
    settle_parts(rows_n - 1)
    dens_load.wait()
    for u in range(gpr):
        rows = slice(u * HALF, (u + 1) * HALF)
        pltpu.make_async_copy(php_v.at[rows], php_out.at[rows], out_s.at[u]).wait()


def hand_over(dens_in, php_in, dens_out, php_out, dens_v, php_v, sems):
    into, out = [], []
    for k, (src, held, dst) in enumerate(((php_in, php_v, php_out), (dens_in, dens_v, dens_out))):
        rows = src.shape[0] // PIECES
        for n in range(PIECES):
            part = slice(n * rows, (n + 1) * rows)
            into.append(pltpu.make_async_copy(src.at[part], held.at[part], sems.at[0, k, n]))
            out.append(pltpu.make_async_copy(held.at[part], dst.at[part], sems.at[1, k, n]))
    for copy in into:
        copy.start()
    for first, second in zip(into, out):
        first.wait()
        second.start()
    for copy in out:
        copy.wait()


def per_device(hamiltonian, pattern, tile_lists, orders, shift):
    rows_n = lax.axis_size("row")
    cols_n = lax.axis_size("col")
    high, wide = hamiltonian.shape
    gpr = high // HALF
    groups = rows_n * gpr
    width = wide // rows_n
    pairs_n = cols_n // 2
    solvers = tile_lists.shape[0]
    blocks = pattern.shape[0]
    dma = pltpu.SemaphoreType.DMA
    smem = pltpu.SMEM
    hbm = pl.BlockSpec(memory_space=pltpu.HBM)
    order = rows_n * high
    scratch = [
        pltpu.VMEM((cols_n, order // TILE, TILE, wide), BF),
        pltpu.VMEM((SPAN, SPAN), BF),
        pltpu.VMEM((SPAN, SPAN), BF),
        pltpu.VMEM((SPAN, SPAN), BF),
        pltpu.VMEM((MAXT, width, TILE), BF),
        pltpu.VMEM((groups, wide, TILE), BF),
        pltpu.VMEM((cols_n, gpr, wide, TILE), BF),
        pltpu.VMEM((groups, wide, HALF), BF),
        pltpu.VMEM((order, high), BF),
        pltpu.VMEM((wide, order), F32),
        pltpu.VMEM((wide, order), BF),
    ]
    results = pl.pallas_call(
        functools.partial(kernel, rows_n, cols_n),
        out_shape=(
            jax.ShapeDtypeStruct((high, wide), BF),
            jax.ShapeDtypeStruct((high, wide), F32),
        ),
        in_specs=[hbm] * 5,
        out_specs=(hbm, hbm),
        scratch_shapes=[
            pltpu.VMEM((high, wide), BF),
            smem((MAXT, solvers), jnp.int32),
            smem((solvers,), jnp.int32),
            smem((blocks, blocks), jnp.int32),
            smem((1,), F32),
            pltpu.VMEM((MAXT, solvers), jnp.int32),
            pltpu.VMEM((groups, solvers), jnp.int32),
            smem((groups, solvers), jnp.int32),
            dma((7,)),
            pltpu.VMEM((high, wide), BF),
            pltpu.VMEM((high, wide), F32),
            dma((gpr + 1,)),
            *scratch,
            *[dma((rows_n * TPC,))] * 3,
            dma((pairs_n,)), dma, dma((rows_n, 2)), *[dma((rows_n,))] * 3,
            *[dma((pairs_n, rows_n * TPC))] * 4,
            *[dma((rows_n, rows_n))] * 2,
            *[dma((pairs_n, gpr))] * 4,
        ],
        compiler_params=pltpu.CompilerParams(
            collective_id=0, has_side_effects=True, vmem_limit_bytes=60000000),
    )(tile_lists.T, orders, pattern, shift, hamiltonian)
    return pl.pallas_call(
        hand_over,
        out_shape=tuple(jax.ShapeDtypeStruct(r.shape, r.dtype) for r in results),
        in_specs=[hbm] * 2,
        out_specs=(hbm, hbm),
        scratch_shapes=[*(pltpu.VMEM(r.shape, r.dtype) for r in results), dma((2, 2, PIECES))],
    )(*results)


def solution(mesh):
    in_specs = (P("row", "col"), P(), P(), P(), P())
    out_specs = (P("row", "col"), P("row", "col"))
    return jax.shard_map(
        per_device, mesh=mesh, in_specs=in_specs, out_specs=out_specs, check_vma=False
    )
```
